128 devices in a mesh: gx: 8 (over y, core), gy: 16 (over z, x).
Axes of the slice: x: 4, y: 4, z: 4, core: 2. Of those that a mesh axis runs over, the one named last changes fastest.
Arguments:
- density: bfloat16 [8, 16, 256, 256], P('gx', 'gy'), may hold values from -0.359375 to 0.359375
- neighbours: int32 [8, 16, 256, 24], P('gx', 'gy'), may hold values from 0 to 2303
- correlations: bfloat16 [8, 16, 256, 34560], P('gx', 'gy'), may hold values from -1.5 to 1.5
- weight_first: bfloat16 [8100, 256], replicated, may hold values from -0.0625 to 0.0625
- bias_first: float32 [256], replicated, may hold values from -3 to 3
- weight_second: bfloat16 [256, 256], replicated, may hold values from -0.375 to 0.375
- bias_second: float32 [256], replicated, may hold values from -3 to 3
- weight_third: bfloat16 [256, 256], replicated, may hold values from -0.375 to 0.375
- bias_third: float32 [256], replicated, may hold values from -3 to 3
- readout: float32 [256], replicated, may hold values from -1.5 to 1.5
- destination: int32 [8, 16, 256, 1], P('gx', 'gy'), may hold values from 0 to 127; in each aligned block of 256 rows (0 to 255, 256 to 511, ..., all dimensions but the last counted through in order) at most 4 rows name the same one
Outputs:
- energy: float32 [8, 16, 256], P('gx', 'gy')
- blocks: float32 [128, 128, 4, 256], P(('gx', 'gy'))
The draws below stay inside these ranges and needn't reach their ends.
Inputs may be any that keep to these rules, and one draw needn't show every extreme that they name: `neighbours`: index n names atom n % 256 of the domain at offset (n // 256 // 3 - 1, n // 256 % 3 - 1) along gx and gy, wrapping around. Devices are numbered gx-major. At most 4 atoms of one domain share a destination, and in every draw some domain has exactly 4 atoms with one destination.
All inputs are finite; a program needn't handle non-finite values.
Results may differ from the reference program's by a relative error of at most 0.0085.
Values may be sent and summed in bfloat16 or wider, within the bound.
A program may use at most 256 MiB of HBM per device.

```python
import math
import jax
import jax.numpy as jnp
import numpy as np
from jax import lax

NPROJ = 90
NORB = 16
HID = 256
K = 24
A_DEV = 256
CAP = 4
N_GX = 8
N_GY = 16
DEVICES = 128


def set_ends(entries, rng, smallest, top_value):
    longest = entries.shape.index(max(entries.shape))
    spots = []
    for shift in (0, 1):
        where = [jax.random.randint(jax.random.fold_in(rng, axis), (), 0, length) for axis, length in enumerate(entries.shape)]
        where[longest] = (where[longest] + shift) % entries.shape[longest]
        spots.append(tuple(where))
    return entries.at[spots[0]].set(smallest).at[spots[1]].set(top_value)


def level_of(key, dims, pieces, low, top_value):
    def one(dim, shards_of):
        steps = jax.random.uniform(jax.random.fold_in(jax.random.fold_in(key, 6), dim), (shards_of,), jnp.float32, low / len(pieces), top_value / len(pieces))
        return jnp.repeat(jnp.exp(steps), dims[dim] // shards_of).reshape((-1,) + (1,) * (len(dims) - dim - 1))

    loudness = one(*pieces[0])
    for cut in pieces[1:]:
        loudness = loudness * one(*cut)
    return loudness


def routed_block(rng, own, number, rows, amount, top, reach, lean):
    order = jax.random.permutation(rng, amount)
    packed, usual = load_shares(amount, rows * top, reach, lean, True), load_shares(amount, rows * top, reach, lean, False)
    places = jnp.arange(amount)

    def named(sizes, rotation):
        used = int((sizes > 0).sum())
        fixed = max(1, used // 4)
        passed = fixed + (places - fixed + rotation * (used - fixed)) % max(1, amount - fixed)
        return jnp.zeros((amount,), jnp.int32).at[order[jnp.where(places < fixed, places, passed)]].set(jnp.asarray(sizes, jnp.int32))

    sizes = jnp.where(number % 4 == 0, named(packed, number // 4), named(usual, number - number // 4 - 1))
    mixed = jax.random.permutation(jax.random.fold_in(own, 3), amount)
    source_of, receiver = mixed[0:amount // 2 * 2:2], mixed[1:amount // 2 * 2:2]
    room = jnp.minimum(sizes[source_of] - 1, reach - sizes[receiver]) // 2
    room = jnp.where((source_of == order[0]) | (receiver == order[0]) | (sizes[receiver] == 0), 0, jnp.maximum(room, 0))
    passed = jax.random.randint(jax.random.fold_in(own, 4), (amount // 2,), 0, 1 << 20) % (room + 1)
    sizes = sizes.at[source_of].add(-passed).at[receiver].add(passed)
    labels = jnp.searchsorted(jnp.cumsum(sizes), jnp.arange(rows * top), side="right").astype(jnp.int32)
    grid = labels.reshape(top, rows).T
    grid = grid[jax.random.permutation(jax.random.fold_in(own, 1), rows)]
    rotation = jax.random.randint(jax.random.fold_in(own, 2), (rows, 1), 0, top)
    return jnp.take_along_axis(grid, (jnp.arange(top)[None, :] + rotation) % top, axis=1)


def load_shares(amount, total, reach, lean, full):
    portions = [(1 << 20) // math.isqrt(grade ** lean) + 1 for grade in range(1, amount + 1)]
    largest = reach if full else min(reach, max(-(-total // amount), total * portions[0] // sum(portions)))
    least = 1 if total - largest >= amount - 1 else 0
    counts, spare = [largest] + [least] * (amount - 1), total - largest - least * (amount - 1)
    while spare > 0:
        candidates = [i for i in range(1, amount) if counts[i] < largest] or [i for i in range(1, amount) if counts[i] < reach]
        mass, remaining = sum([portions[i] for i in candidates]), spare
        for i in candidates:
            addition = min(reach - counts[i], max(1, remaining * portions[i] // mass), spare)
            counts[i] = counts[i] + addition
            spare = spare - addition
    return np.array(counts)


def centred(key, extent, spread, bound, shards=(), kind=jnp.bfloat16):
    array = spread * jax.random.normal(key, extent, jnp.float32)
    if shards:
        array = array * level_of(key, extent, shards, -0.22, 0.18)
    return jnp.clip(array, -bound, bound).astype(kind)


def setup_inputs(seed: int = 0) -> dict:
    splits = jax.random.split(jax.random.key(seed), 12)
    density = centred(splits[0], (N_GX, N_GY, A_DEV, NORB * NORB), 0.06, 0.359375, ((0, 8), (1, 16)))
    neighbours = set_ends(jax.random.randint(splits[1], (N_GX, N_GY, A_DEV, K), 0, 9 * A_DEV), jax.random.fold_in(splits[1], 1), 0, (9 * A_DEV) - 1).astype(jnp.int32)
    correlations = centred(splits[2], (N_GX, N_GY, A_DEV, NPROJ * K * NORB), NORB ** -0.5, 1.5, ((0, 8), (1, 16)))
    weight_first = centred(splits[3], (NPROJ * NPROJ, HID), (NPROJ * NPROJ) ** -0.5, 0.0625)
    bias_first = centred(splits[4], (HID,), 0.5, 3.0, (), jnp.float32)
    weight_second = centred(splits[5], (HID, HID), HID ** -0.5, 0.375)
    bias_second = centred(splits[6], (HID,), 0.5, 3.0, (), jnp.float32)
    weight_third = centred(splits[7], (HID, HID), HID ** -0.5, 0.375)
    bias_third = centred(splits[8], (HID,), 0.5, 3.0, (), jnp.float32)
    readout = centred(splits[9], (HID,), 0.25, 1.5, (), jnp.float32)
    destination_keys = jax.random.split(jax.random.fold_in(splits[10], 1), N_GX * N_GY * A_DEV // A_DEV)
    destination_turns = jax.random.permutation(jax.random.fold_in(splits[10], 3), N_GX * N_GY * A_DEV // A_DEV)
    destination = jax.vmap(lambda own, number: routed_block(jax.random.fold_in(splits[10], 2), own, number, A_DEV, DEVICES, 1, CAP, 2))(destination_keys, destination_turns).reshape((N_GX, N_GY, A_DEV, 1))
    return {"density": density, "neighbours": neighbours, "correlations": correlations, "weight_first": weight_first, "bias_first": bias_first, "weight_second": weight_second, "bias_second": bias_second, "weight_third": weight_third, "bias_third": bias_third, "readout": readout, "destination": destination}


def network(descriptor, weight_first, bias_first, weight_second, bias_second, weight_third, bias_third, readout):
    pre_first = jnp.dot(descriptor, weight_first, preferred_element_type=jnp.float32) + bias_first
    act_first = jnp.tanh(pre_first)
    pre_second = jnp.dot(act_first.astype(jnp.bfloat16), weight_second, preferred_element_type=jnp.float32) + bias_second
    act_second = act_first + jnp.tanh(pre_second)
    pre_third = jnp.dot(act_second.astype(jnp.bfloat16), weight_third, preferred_element_type=jnp.float32) + bias_third
    act_third = act_second + jnp.tanh(pre_third)
    energy = jnp.sum(act_third * readout, axis=-1)
    grad_third = (readout * (1.0 - jnp.tanh(pre_third) ** 2)).astype(jnp.bfloat16)
    back_second = readout + jnp.dot(grad_third, weight_third.T, preferred_element_type=jnp.float32)
    grad_second = (back_second * (1.0 - jnp.tanh(pre_second) ** 2)).astype(jnp.bfloat16)
    back_first = back_second + jnp.dot(grad_second, weight_second.T, preferred_element_type=jnp.float32)
    grad_first = (back_first * (1.0 - act_first ** 2)).astype(jnp.bfloat16)
    slope = jnp.dot(grad_first, weight_first.T, preferred_element_type=jnp.float32).astype(jnp.bfloat16)
    return energy, slope


def reference(density, neighbours, correlations, weight_first, bias_first, weight_second, bias_second, weight_third, bias_third, readout, destination):
    domains = N_GX * N_GY
    shifted = []
    for offset_x in range(3):
        for offset_y in range(3):
            shifted.append(jnp.roll(density, (1 - offset_x, 1 - offset_y), (0, 1)))
    extended = jnp.stack(shifted, axis=2).reshape(domains, 9 * A_DEV, NORB * NORB)
    nbr_flat = neighbours.reshape(domains, A_DEV, K)
    over_flat = correlations.reshape(domains, A_DEV, NPROJ * K * NORB)

    def domain_work(inputs):
        ext_local, nbr_local, over_local = inputs
        gathered = ext_local[nbr_local].reshape(A_DEV, K, NORB, NORB).astype(jnp.float32)
        projector = over_local.reshape(A_DEV, NPROJ, K, NORB).transpose(0, 2, 1, 3).astype(jnp.float32)
        partial_value = jnp.einsum('akpo,akoq->akpq', projector, gathered).astype(jnp.bfloat16)
        descriptor = jnp.einsum('akpq,akrq->apr', partial_value.astype(jnp.float32), projector).astype(jnp.bfloat16)
        energy, slope = network(descriptor.reshape(A_DEV, NPROJ * NPROJ), weight_first, bias_first, weight_second, bias_second, weight_third, bias_third, readout)
        slope = slope.reshape(A_DEV, NPROJ, NPROJ).astype(jnp.float32)
        lifted = jnp.einsum('apr,akrq->akpq', slope, projector).astype(jnp.bfloat16)
        pair_blocks = jnp.einsum('akpo,akpq->akoq', projector, lifted.astype(jnp.float32))
        summed = jax.ops.segment_sum(pair_blocks.reshape(A_DEV * K, NORB * NORB), nbr_local.reshape(-1), num_segments=9 * A_DEV)
        return energy, summed.reshape(3, 3, A_DEV, NORB * NORB)

    energy, contrib = lax.map(domain_work, (extended, nbr_flat, over_flat))
    contrib = contrib.reshape(N_GX, N_GY, 3, 3, A_DEV, NORB * NORB)
    hamilton = jnp.zeros((N_GX, N_GY, A_DEV, NORB * NORB), jnp.float32)
    for offset_x in range(3):
        for offset_y in range(3):
            hamilton = hamilton + jnp.roll(contrib[:, :, offset_x, offset_y], (offset_x - 1, offset_y - 1), (0, 1))
    hamilton = hamilton.reshape(domains, A_DEV, NORB * NORB)
    target = destination.reshape(domains, A_DEV)
    same = target[:, :, None] == target[:, None, :]
    order = jnp.arange(A_DEV, dtype=jnp.int32)
    earlier = order[None, :] < order[:, None]
    slot = jnp.sum(jnp.logical_and(same, earlier[None]).astype(jnp.int32), axis=2).astype(jnp.int32)
    position = (target * CAP + slot).astype(jnp.int32)
    source = jnp.broadcast_to(jnp.arange(domains, dtype=jnp.int32)[:, None], (domains, A_DEV))
    buffer = jnp.zeros((domains, domains * CAP, NORB * NORB), jnp.float32).at[source, position].set(hamilton)
    blocks = buffer.reshape(domains, domains, CAP, NORB * NORB).transpose(1, 0, 2, 3)
    return energy.reshape(N_GX, N_GY, A_DEV), blocks
```

```python
import functools
import jax, jax.numpy as jnp
from jax import lax
from jax.experimental import pallas as pl
from jax.experimental.pallas import tpu as pltpu
from jax.sharding import PartitionSpec as P
F32, BF = jnp.float32, jnp.bfloat16
NP, NK, NO, H, A = 90, 24, 16, 256, 256
PR = 96
G = 16
NT = (((1,), (1,)), ((), ()))

def dot(a, b):
    return jnp.dot(a, b, preferred_element_type=F32)
def dot_nt(a, b):
    return lax.dot_general(a, b, NT, preferred_element_type=F32)

def diag(x, y):
    z = jnp.zeros_like(x)
    return jnp.concatenate([jnp.concatenate([x, z], 1), jnp.concatenate([z, y], 1)], 0)

def k1_body(unroll, nbr, ext, sel, corr, mask, d_ref, ot_ref, table, tmp):
    step = pl.program_id(0)
    @pl.when(step == 0)
    def _():
        tmp[pl.ds(270 * 16, 18 * 16), :] = jnp.zeros((18 * 16, 128), F32)
        @pl.loop(0, 9)
        def _(b):
            for o in range(16):
                t = dot(ext[pl.ds(pl.multiple_of(b * 256, 256), 256), :], sel[:, o * 128:(o + 1) * 128])
                tmp[pl.ds(o, 256, stride=16), :] = t
            table[pl.ds(b * 256, 256)] = tmp[pl.ds(0, 4096), :].reshape(256, 16, 128).astype(BF)
    @pl.loop(0, 10)
    def _(c):
        for r in range(27):
            x = corr[:, pl.ds(pl.multiple_of((c * 27 + r) * 128, 128), 128)].astype(F32)
            tmp[pl.ds(pl.multiple_of((c * 27 + r) * 16, 16), 16), :] = x
    eye = (lax.broadcasted_iota(jnp.int32, (128, 256), 0) == lax.broadcasted_iota(jnp.int32, (128, 256), 1) % 128).astype(BF)
    pad = jnp.zeros((128 - PR, 128), BF)
    d2 = d_ref.reshape(PR * G, 128)
    def pair(i):
        d = jnp.zeros((PR, 256), F32)
        for j in range(3):
            o = [tmp[pl.ds(j * 16 + 2 * i + h, PR, stride=48), :].astype(BF) for h in range(2)]
            bd = []
            for h in range(2):
                base = (step * G + 2 * i + h) * NK + 8 * j
                bd.append(jnp.concatenate([table[nbr[base + kk]] * mask[kk] for kk in range(8)], 0))
            p = dot(jnp.concatenate(o, 1), diag(*bd)).astype(BF)
            rhs = diag(*[jnp.concatenate([v, pad], 0) for v in o])
            r = dot_nt(jnp.concatenate([p, eye], 0), rhs)
            d = d + r[:PR]
            ot_ref[i, j * 128:(j + 1) * 128, :] = r[PR:].astype(BF)
        for h in range(2):
            d2[pl.ds(2 * i + h, PR, stride=G), :] = d[:, h * 128:(h + 1) * 128]
    @pl.loop(0, G // 2 // unroll)
    def _(i):
        for u in range(unroll):
            pair(i * unroll + u)

def k1(nbr, ext, sel, corr, mask, unroll=1):
    return pl.pallas_call(
        functools.partial(k1_body, unroll),
        grid_spec=pltpu.PrefetchScalarGridSpec(
            num_scalar_prefetch=1, grid=(A // G,),
            in_specs=[pl.BlockSpec((9 * A, 256), lambda s, n: (0, 0)),
                      pl.BlockSpec((256, 2048), lambda s, n: (0, 0)),
                      pl.BlockSpec((G, 34560), lambda s, n: (s, 0)),
                      pl.BlockSpec((8, 16, 128), lambda s, n: (0, 0, 0))],
            out_specs=[pl.BlockSpec((PR, G, 128), lambda s, n: (0, s, 0)),
                       pl.BlockSpec((G // 2, 384, 256), lambda s, n: (s, 0, 0))],
            scratch_shapes=[pltpu.VMEM((9 * A, 16, 128), BF), pltpu.VMEM((288 * 16, 128), F32)]),
        out_shape=[jax.ShapeDtypeStruct((PR, A, 128), F32), jax.ShapeDtypeStruct((A // 2, 384, 256), BF)],
        compiler_params=pltpu.CompilerParams(vmem_limit_bytes=60 << 20, dimension_semantics=("arbitrary",)),
        name="descriptor",
    )(nbr, ext, sel, corr, mask)

def consts():
    i = jnp.arange(256)[:, None]; c = jnp.arange(2048)[None]
    sel = ((i // 16 == c // 128) & (i % 16 == c % 16)).astype(BF)
    k = jnp.arange(8)[:, None, None]; l = jnp.arange(128)[None, None]
    mask = jnp.broadcast_to((l // 16 == k), (8, 16, 128)).astype(BF)
    return sel, mask

def relay(corr):
    return corr.reshape(256, 34560)

PC = 16
def k2_body(d_ref, w1, b1, w2, b2, w3, b3, ro, e_ref, s_ref, acc, grad):
    phase, c = pl.program_id(0), pl.program_id(1)
    last = pl.num_programs(1) - 1
    @pl.when(phase == 0)
    def _():
        t = jnp.zeros((A, H), F32)
        for p in range(0, PC, 2):
            x = jnp.concatenate([d_ref[p], d_ref[p + 1]], 1).astype(BF)
            t = t + dot(x, w1[p:p + 2].reshape(256, H))
        acc[...] = jnp.where(c == 0, 0.0, acc[...]) + t
        @pl.when(c == last)
        def _():
            act1 = jnp.tanh(acc[...] + b1[...])
            th2 = jnp.tanh(dot(act1.astype(BF), w2[...]) + b2[...])
            act2 = act1 + th2
            th3 = jnp.tanh(dot(act2.astype(BF), w3[...]) + b3[...])
            e_ref[...] = jnp.sum((act2 + th3) * ro[...], axis=1, keepdims=True)
            g3 = (ro[...] * (1.0 - th3 * th3)).astype(BF)
            back2 = ro[...] + dot_nt(g3, w3[...])
            g2 = (back2 * (1.0 - th2 * th2)).astype(BF)
            back1 = back2 + dot_nt(g2, w2[...])
            grad[...] = (back1 * (1.0 - act1 * act1)).astype(BF)
    @pl.when(phase == 1)
    def _():
        for p in range(0, PC, 2):
            t = dot_nt(grad[...], w1[p:p + 2].reshape(256, H))
            s_ref[p] = t[:, :128]
            s_ref[p + 1] = t[:, 128:]

def k2(d, w1p, b1, w2, b2, w3, b3, ro):
    n = PR // PC
    row = lambda: pl.BlockSpec((1, H), lambda f, c: (0, 0))
    mat = lambda: pl.BlockSpec((H, H), lambda f, c: (0, 0))
    return pl.pallas_call(
        k2_body, grid=(2, n),
        in_specs=[pl.BlockSpec((PC, A, 128), lambda f, c: (jnp.where(f == 0, c, n - 1), 0, 0)),
                  pl.BlockSpec((PC, 128, H), lambda f, c: (c, 0, 0)),
                  row(), mat(), row(), mat(), row(), row()],
        out_specs=[pl.BlockSpec((A, 1), lambda f, c: (0, 0)),
                   pl.BlockSpec((PC, A, 128), lambda f, c: (jnp.where(f == 0, 0, c), 0, 0))],
        scratch_shapes=[pltpu.VMEM((A, H), F32), pltpu.VMEM((A, H), BF)],
        out_shape=[jax.ShapeDtypeStruct((A, 1), F32), jax.ShapeDtypeStruct((PR, A, 128), F32)],
        compiler_params=pltpu.CompilerParams(vmem_limit_bytes=40 << 20),
        name="network",
    )(d, w1p, b1, w2, b2, w3, b3, ro)

def k3_body(unroll, nbr, s_ref, ot_ref, fold, out_ref, acc, lift):
    step = pl.program_id(0)
    @pl.when(step == 0)
    def _():
        @pl.loop(0, 144)
        def _(c):
            acc[pl.ds(c * 16, 16)] = jnp.zeros((16, 16, 128), F32)
    s2 = s_ref.reshape(PR * G, 128)
    pad = jnp.zeros((128 - PR, 128), BF)
    lane = lax.broadcasted_iota(jnp.int32, (16, 128), 1) // 16
    def pair(i):
        s = [jnp.concatenate([s2[pl.ds(2 * i + h, PR, stride=G), :].astype(BF), pad], 0) for h in range(2)]
        lt = dot_nt(ot_ref[i], diag(*s)).astype(BF)
        for j in range(3):
            ot = ot_ref[i, j * 128:(j + 1) * 128, :]
            zero = jnp.zeros((128, 128), BF)
            rhs = jnp.concatenate([jnp.concatenate([ot[:, :128], zero], 1), jnp.concatenate([zero, ot[:, 128:]], 1)], 0)
            r = dot_nt(lt[j * 128:(j + 1) * 128], rhs)
            for h in range(2):
                base = (step * G + 2 * i + h) * NK + 8 * j
                ns = [nbr[base + kk] for kk in range(8)]
                new = [acc[ns[kk]] + r[kk * 16:(kk + 1) * 16, h * 128:(h + 1) * 128] for kk in range(8)]
                for kk in range(8):
                    pltpu.store(acc.at[ns[kk]], new[kk], mask=lane == kk)
    @pl.loop(0, G // 2 // unroll)
    def _(i):
        for u in range(unroll):
            pair(i * unroll + u)
    @pl.when(step == pl.num_programs(0) - 1)
    def _():
        acc2 = acc.reshape(9 * A * 16, 128)
        @pl.loop(0, 9)
        def _(b):
            t = jnp.zeros((256, 256), F32)
            for q in range(0, 16, 2):
                x = jnp.concatenate([acc2[pl.ds(b * 4096 + q + h, 256, stride=16), :] for h in range(2)], 1).astype(BF)
                t = t + dot(x, fold[q * 128:(q + 2) * 128, :])
            out_ref[pl.ds(pl.multiple_of(b * 256, 256), 256), :] = t.astype(BF)

def k3(nbr, s, ot, fold, unroll=1):
    return pl.pallas_call(
        functools.partial(k3_body, unroll),
        grid_spec=pltpu.PrefetchScalarGridSpec(
            num_scalar_prefetch=1, grid=(A // G,),
            in_specs=[pl.BlockSpec((PR, G, 128), lambda s, n: (0, s, 0)),
                      pl.BlockSpec((G // 2, 384, 256), lambda s, n: (s, 0, 0)),
                      pl.BlockSpec((2048, 256), lambda s, n: (0, 0))],
            out_specs=pl.BlockSpec((9 * A, 256), lambda s, n: (0, 0)),
            scratch_shapes=[pltpu.VMEM((9 * A, 16, 128), F32), pltpu.VMEM((384, 256), BF)]),
        out_shape=jax.ShapeDtypeStruct((9 * A, 256), BF),
        compiler_params=pltpu.CompilerParams(vmem_limit_bytes=60 << 20),
        name="hamilton",
    )(nbr, s, ot, fold)

def fold_of():
    i = jnp.arange(2048)[:, None]; c = jnp.arange(256)[None]
    return ((i // 128 == c % 16) & (i % 16 == c // 16)).astype(BF)

def w1_of(w):
    return jnp.pad(w.reshape(NP, NP, H), ((0, PR - NP), (0, 128 - NP), (0, 0)))


def shifted(value, axis, steps):
    count = lax.axis_size(axis)
    return lax.ppermute(value, axis, [(s, (s + steps) % count) for s in range(count)])


def padded(block, sides):
    for axis, dim in sides:
        block = jnp.concatenate([shifted(block, axis, 1), block, shifted(block, axis, -1)], axis=dim)
    return block


def on_device(density, neighbours, correlations, weight_first, bias_first, weight_second, bias_second,
              weight_third, bias_third, readout, destination):
    sel, mask = consts()
    nbr = neighbours.reshape(A * NK)
    ext = padded(density, (("gy", 1), ("gx", 0))).reshape(9 * A, 256)
    row = lambda v: v.reshape(1, H)
    d, ot = k1(nbr, ext, sel, relay(correlations), mask, 4)
    energy, slope = k2(d, w1_of(weight_first), row(bias_first), weight_second, row(bias_second),
                       weight_third, row(bias_third), row(readout))
    part = k3(nbr, slope, ot, fold_of(), 1).reshape(3, 3, A, 256)
    folded = part[1].astype(F32)
    for s in (1, -1):
        folded = folded + shifted(part[1 + s], "gx", s).astype(F32)
    hamilton = folded[1]
    for s in (1, -1):
        hamilton = hamilton + shifted(folded[1 + s].astype(BF), "gy", s).astype(F32)
    target = destination.reshape(A)
    order = jnp.arange(A, dtype=jnp.int32)
    earlier = (target[:, None] == target[None, :]) & (order[None, :] < order[:, None])
    position = target * 4 + jnp.sum(earlier.astype(jnp.int32), axis=1)
    chosen = (jnp.arange(512, dtype=jnp.int32)[:, None] == position[None, :]).astype(BF)
    outgoing = dot(chosen, hamilton.astype(BF)).astype(BF).reshape(128, 4, 256)
    received = lax.all_to_all(outgoing, ("gx", "gy"), split_axis=0, concat_axis=0, tiled=True)
    return energy.reshape(1, 1, A), received[None].astype(F32)


def solution(mesh):
    own = P("gx", "gy", None, None)
    return jax.shard_map(
        on_device,
        mesh=mesh,
        in_specs=(own, own, own, P(), P(), P(), P(), P(), P(), P(), own),
        out_specs=(P("gx", "gy", None), P(("gx", "gy"), None, None, None)),
        check_vma=False,
    )
```

```python
import functools
import jax, jax.numpy as jnp
from jax import lax
from jax.experimental import pallas as pl
from jax.experimental.pallas import tpu as pltpu
from jax.sharding import PartitionSpec as P
F32, BF = jnp.float32, jnp.bfloat16
NP, NK, NO, H, A = 90, 24, 16, 256, 256
PR = 96
G = 16
NT = (((1,), (1,)), ((), ()))

def dot(a, b):
    return jnp.dot(a, b, preferred_element_type=F32)
def dot_nt(a, b):
    return lax.dot_general(a, b, NT, preferred_element_type=F32)

def diag(x, y):
    z = jnp.zeros_like(x)
    return jnp.concatenate([jnp.concatenate([x, z], 1), jnp.concatenate([z, y], 1)], 0)

def k1_body(unroll, nbr, ext, sel, corr, mask, d_ref, o_ref, table, tmp):
    step = pl.program_id(0)
    @pl.when(step == 0)
    def _():
        tmp[pl.ds(270 * 16, 18 * 16), :] = jnp.zeros((18 * 16, 128), F32)
        @pl.loop(0, 9)
        def _(b):
            for o in range(16):
                t = dot(ext[pl.ds(pl.multiple_of(b * 256, 256), 256), :], sel[:, o * 128:(o + 1) * 128])
                tmp[pl.ds(o, 256, stride=16), :] = t
            table[pl.ds(b * 256, 256)] = tmp[pl.ds(0, 4096), :].reshape(256, 16, 128).astype(BF)
    @pl.loop(0, 10)
    def _(c):
        for r in range(27):
            x = corr[:, pl.ds(pl.multiple_of((c * 27 + r) * 128, 128), 128)].astype(F32)
            tmp[pl.ds(pl.multiple_of((c * 27 + r) * 16, 16), 16), :] = x
    pad = jnp.zeros((128 - PR, 128), BF)
    d2 = d_ref.reshape(PR * G, 128)
    def bdiag(i, h, j):
        base = (step * G + 2 * i + h) * NK + 8 * j
        return jnp.concatenate([table[nbr[base + kk]] * mask[kk] for kk in range(8)], 0)
    def pair(i):
        o = [[tmp[pl.ds(j * 16 + 2 * i + h, PR, stride=48), :].astype(BF) for j in range(3)] for h in range(2)]
        ot = [[jnp.concatenate([o[h][j], pad], 0).T for j in range(3)] for h in range(2)]
        p = []
        for j in range(3):
            both = jnp.concatenate([o[0][j], o[1][j]], 1)
            o_ref[i, :, j * 256:(j + 1) * 256] = both
            p.append(dot(both, diag(bdiag(i, 0, j), bdiag(i, 1, j))).astype(BF))
        d = dot(jnp.concatenate(p, 1), jnp.concatenate([diag(ot[0][j], ot[1][j]) for j in range(3)], 0))
        for h in range(2):
            d2[pl.ds(2 * i + h, PR, stride=G), :] = d[:, h * 128:(h + 1) * 128]
    @pl.loop(0, G // 2 // unroll)
    def _(i):
        for u in range(unroll):
            pair(i * unroll + u)

def k1(nbr, ext, sel, corr, mask, unroll=1):
    return pl.pallas_call(
        functools.partial(k1_body, unroll),
        grid_spec=pltpu.PrefetchScalarGridSpec(
            num_scalar_prefetch=1, grid=(A // G,),
            in_specs=[pl.BlockSpec((9 * A, 256), lambda s, n: (0, 0)),
                      pl.BlockSpec((256, 2048), lambda s, n: (0, 0)),
                      pl.BlockSpec((G, 34560), lambda s, n: (s, 0)),
                      pl.BlockSpec((8, 16, 128), lambda s, n: (0, 0, 0))],
            out_specs=[pl.BlockSpec((PR, G, 128), lambda s, n: (0, s, 0)),
                       pl.BlockSpec((G // 2, PR, 768), lambda s, n: (s, 0, 0))],
            scratch_shapes=[pltpu.VMEM((9 * A, 16, 128), BF), pltpu.VMEM((288 * 16, 128), F32)]),
        out_shape=[jax.ShapeDtypeStruct((PR, A, 128), F32), jax.ShapeDtypeStruct((A // 2, PR, 768), BF)],
        compiler_params=pltpu.CompilerParams(vmem_limit_bytes=60 << 20, dimension_semantics=("arbitrary",)),
        name="descriptor",
    )(nbr, ext, sel, corr, mask)

def consts():
    i = jnp.arange(256)[:, None]; c = jnp.arange(2048)[None]
    sel = (((i >> 4) == (c >> 7)) & ((i & 15) == (c & 15))).astype(BF)
    k = jnp.arange(8)[:, None, None]; l = jnp.arange(128)[None, None]
    mask = jnp.broadcast_to(((l >> 4) == k), (8, 16, 128)).astype(BF)
    return sel, mask

def relay(corr):
    return corr.reshape(256, 34560)

PC = 16
def k2_body(d_ref, w1, b1, w2, b2, w3, b3, ro, e_ref, s_ref, acc, grad, rows):
    phase, c = pl.program_id(0), pl.program_id(1)
    last = pl.num_programs(1) - 1
    pad = jnp.zeros((128 - PR, H), BF)
    inside = c * (PC * NP) + lax.broadcasted_iota(jnp.int32, (PC * NP, H), 0) < NP * NP
    rows[:PC * NP, :] = jnp.where(inside, w1[...].astype(F32), 0.0)
    rows[PC * NP:, :] = jnp.zeros((8, H), F32)
    def weights(p):
        w = [rows[NP * v:NP * v + PR, :].astype(BF) for v in (p, p + 1)]
        return jnp.concatenate([w[0], pad, w[1], pad], 0)
    @pl.when(phase == 0)
    def _():
        t = jnp.zeros((A, H), F32)
        for p in range(0, PC, 2):
            x = jnp.concatenate([d_ref[p], d_ref[p + 1]], 1).astype(BF)
            t = t + dot(x, weights(p))
        acc[...] = jnp.where(c == 0, 0.0, acc[...]) + t
        @pl.when(c == last)
        def _():
            act1 = jnp.tanh(acc[...] + b1[...])
            th2 = jnp.tanh(dot(act1.astype(BF), w2[...]) + b2[...])
            act2 = act1 + th2
            th3 = jnp.tanh(dot(act2.astype(BF), w3[...]) + b3[...])
            e_ref[...] = jnp.sum((act2 + th3) * ro[...], axis=1, keepdims=True)
            g3 = (ro[...] * (1.0 - th3 * th3)).astype(BF)
            back2 = ro[...] + dot_nt(g3, w3[...])
            g2 = (back2 * (1.0 - th2 * th2)).astype(BF)
            back1 = back2 + dot_nt(g2, w2[...])
            grad[...] = (back1 * (1.0 - act1 * act1)).astype(BF)
    @pl.when(phase == 1)
    def _():
        for p in range(0, PC, 2):
            t = dot_nt(grad[...], weights(p))
            s_ref[p] = t[:, :128]
            s_ref[p + 1] = t[:, 128:]

def k2(d, w1, b1, w2, b2, w3, b3, ro):
    n = PR // PC
    row = lambda: pl.BlockSpec((1, H), lambda f, c: (0, 0))
    mat = lambda: pl.BlockSpec((H, H), lambda f, c: (0, 0))
    return pl.pallas_call(
        k2_body, grid=(2, n),
        in_specs=[pl.BlockSpec((PC, A, 128), lambda f, c: (jnp.where(f == 0, c, n - 1), 0, 0)),
                  pl.BlockSpec((PC * NP, H), lambda f, c: (c, 0)),
                  row(), mat(), row(), mat(), row(), row()],
        out_specs=[pl.BlockSpec((A, 1), lambda f, c: (0, 0)),
                   pl.BlockSpec((PC, A, 128), lambda f, c: (jnp.where(f == 0, 0, c), 0, 0))],
        scratch_shapes=[pltpu.VMEM((A, H), F32), pltpu.VMEM((A, H), BF), pltpu.VMEM((PC * NP + 8, H), F32)],
        out_shape=[jax.ShapeDtypeStruct((A, 1), F32), jax.ShapeDtypeStruct((PR, A, 128), F32)],
        compiler_params=pltpu.CompilerParams(vmem_limit_bytes=40 << 20),
        name="network",
    )(d, w1, b1, w2, b2, w3, b3, ro)

def k3_body(unroll, nbr, s_ref, o_ref, fold, out_ref, acc):
    step = pl.program_id(0)
    @pl.when(step == 0)
    def _():
        @pl.loop(0, 144)
        def _(c):
            acc[pl.ds(c * 16, 16)] = jnp.zeros((16, 16, 128), F32)
    s2 = s_ref.reshape(PR * G, 128)
    pad = jnp.zeros((128 - PR, 128), BF)
    lane = lax.broadcasted_iota(jnp.int32, (16, 128), 1) // 16
    def pair(i):
        st = [jnp.concatenate([s2[pl.ds(2 * i + h, PR, stride=G), :].astype(BF), pad], 0).T for h in range(2)]
        o = [[jnp.concatenate([o_ref[i, :, j * 256 + h * 128:j * 256 + h * 128 + 128], pad], 0) for j in range(3)] for h in range(2)]
        ot = jnp.concatenate([jnp.concatenate([o[0][j].T, o[1][j].T], 1) for j in range(3)], 0)
        lt = dot(ot, diag(*st)).astype(BF)
        for j in range(3):
            r = dot(lt[j * 128:(j + 1) * 128], diag(o[0][j], o[1][j]))
            for h in range(2):
                base = (step * G + 2 * i + h) * NK + 8 * j
                ns = [nbr[base + kk] for kk in range(8)]
                new = [acc[ns[kk]] + r[kk * 16:(kk + 1) * 16, h * 128:(h + 1) * 128] for kk in range(8)]
                for kk in range(8):
                    pltpu.store(acc.at[ns[kk]], new[kk], mask=lane == kk)
    @pl.loop(0, G // 2 // unroll)
    def _(i):
        for u in range(unroll):
            pair(i * unroll + u)
    @pl.when(step == pl.num_programs(0) - 1)
    def _():
        acc2 = acc.reshape(9 * A * 16, 128)
        @pl.loop(0, 9)
        def _(b):
            t = jnp.zeros((256, 256), F32)
            for q in range(0, 16, 2):
                x = jnp.concatenate([acc2[pl.ds(b * 4096 + q + h, 256, stride=16), :] for h in range(2)], 1).astype(BF)
                t = t + dot(x, fold[q * 128:(q + 2) * 128, :])
            out_ref[pl.ds(pl.multiple_of(b * 256, 256), 256), :] = t.astype(BF)

def k3(nbr, s, ot, fold, unroll=1):
    return pl.pallas_call(
        functools.partial(k3_body, unroll),
        grid_spec=pltpu.PrefetchScalarGridSpec(
            num_scalar_prefetch=1, grid=(A // G,),
            in_specs=[pl.BlockSpec((PR, G, 128), lambda s, n: (0, s, 0)),
                      pl.BlockSpec((G // 2, PR, 768), lambda s, n: (s, 0, 0)),
                      pl.BlockSpec((2048, 256), lambda s, n: (0, 0))],
            out_specs=pl.BlockSpec((9 * A, 256), lambda s, n: (0, 0)),
            scratch_shapes=[pltpu.VMEM((9 * A, 16, 128), F32)]),
        out_shape=jax.ShapeDtypeStruct((9 * A, 256), BF),
        compiler_params=pltpu.CompilerParams(vmem_limit_bytes=60 << 20),
        name="hamilton",
    )(nbr, s, ot, fold)

def fold_of():
    i = jnp.arange(2048)[:, None]; c = jnp.arange(256)[None]
    return (((i >> 7) == (c & 15)) & ((i & 15) == (c >> 4))).astype(BF)


def shifted(value, axis, steps):
    count = lax.axis_size(axis)
    return lax.ppermute(value, axis, [(s, (s + steps) % count) for s in range(count)])


def padded(block, sides):
    for axis, dim in sides:
        block = jnp.concatenate([shifted(block, axis, 1), block, shifted(block, axis, -1)], axis=dim)
    return block


def on_device(density, neighbours, correlations, weight_first, bias_first, weight_second, bias_second,
              weight_third, bias_third, readout, destination):
    sel, mask = consts()
    nbr = neighbours.reshape(A * NK)
    ext = padded(density, (("gy", 1), ("gx", 0))).reshape(9 * A, 256)
    row = lambda v: v.reshape(1, H)
    d, ot = k1(nbr, ext, sel, relay(correlations), mask, 8)
    energy, slope = k2(d, weight_first, row(bias_first), weight_second, row(bias_second),
                       weight_third, row(bias_third), row(readout))
    part = k3(nbr, slope, ot, fold_of(), 8).reshape(3, 3, A, 256)
    folded = part[1].astype(F32)
    for s in (1, -1):
        folded = folded + shifted(part[1 + s], "gx", s).astype(F32)
    hamilton = folded[1]
    for s in (1, -1):
        hamilton = hamilton + shifted(folded[1 + s].astype(BF), "gy", s).astype(F32)
    target = destination.reshape(A)
    order = jnp.arange(A, dtype=jnp.int32)
    earlier = (target[:, None] == target[None, :]) & (order[None, :] < order[:, None])
    position = target * 4 + jnp.sum(earlier.astype(jnp.int32), axis=1)
    chosen = (jnp.arange(512, dtype=jnp.int32)[:, None] == position[None, :]).astype(BF)
    outgoing = dot(chosen, hamilton.astype(BF)).astype(BF).reshape(128, 4, 256)
    received = lax.all_to_all(outgoing, ("gx", "gy"), split_axis=0, concat_axis=0, tiled=True)
    return energy.reshape(1, 1, A), received[None].astype(F32)


def solution(mesh):
    own = P("gx", "gy", None, None)
    return jax.shard_map(
        on_device,
        mesh=mesh,
        in_specs=(own, own, own, P(), P(), P(), P(), P(), P(), P(), own),
        out_specs=(P("gx", "gy", None), P(("gx", "gy"), None, None, None)),
        check_vma=False,
    )
```

```python
import functools
import jax, jax.numpy as jnp
from jax import lax
from jax.experimental import pallas as pl
from jax.experimental.pallas import tpu as pltpu
from jax.sharding import PartitionSpec as P
F32, BF = jnp.float32, jnp.bfloat16
NP, NK, NO, H, A = 90, 24, 16, 256, 256
PR = 96
G = 16
NT = (((1,), (1,)), ((), ()))

def dot(a, b):
    return jnp.dot(a, b, preferred_element_type=F32)
def dot_nt(a, b):
    return lax.dot_general(a, b, NT, preferred_element_type=F32)

def diag(x, y):
    z = jnp.zeros_like(x)
    return jnp.concatenate([jnp.concatenate([x, z], 1), jnp.concatenate([z, y], 1)], 0)

def k1_body(unroll, nbr, ext, sel, corr, mask, d_ref, o_ref, table, tmp):
    step = pl.program_id(0)
    @pl.when(step == 0)
    def _():
        tmp[pl.ds(270 * 16, 18 * 16), :] = jnp.zeros((18 * 16, 128), F32)
        @pl.loop(0, 9)
        def _(b):
            for o in range(16):
                t = dot(ext[pl.ds(pl.multiple_of(b * 256, 256), 256), :], sel[:, o * 128:(o + 1) * 128])
                tmp[pl.ds(o, 256, stride=16), :] = t
            table[pl.ds(b * 256, 256)] = tmp[pl.ds(0, 4096), :].reshape(256, 16, 128).astype(BF)
    @pl.loop(0, 10)
    def _(c):
        for r in range(27):
            x = corr[:, pl.ds(pl.multiple_of((c * 27 + r) * 128, 128), 128)].astype(F32)
            tmp[pl.ds(pl.multiple_of((c * 27 + r) * 16, 16), 16), :] = x
    pad = jnp.zeros((128 - PR, 128), BF)
    d2 = d_ref.reshape(PR * G, 128)
    def bdiag(i, h, j):
        base = (step * G + 2 * i + h) * NK + 8 * j
        return jnp.concatenate([table[nbr[base + kk]] * mask[kk] for kk in range(8)], 0)
    def pair(i):
        o = [[tmp[pl.ds(j * 16 + 2 * i + h, PR, stride=48), :].astype(BF) for j in range(3)] for h in range(2)]
        ot = [[jnp.concatenate([o[h][j], pad], 0).T for j in range(3)] for h in range(2)]
        p = []
        for j in range(3):
            both = jnp.concatenate([o[0][j], o[1][j]], 1)
            o_ref[i, :, j * 256:(j + 1) * 256] = both
            p.append(dot(both, diag(bdiag(i, 0, j), bdiag(i, 1, j))).astype(BF))
        d = dot(jnp.concatenate(p, 1), jnp.concatenate([diag(ot[0][j], ot[1][j]) for j in range(3)], 0))
        for h in range(2):
            d2[pl.ds(2 * i + h, PR, stride=G), :] = d[:, h * 128:(h + 1) * 128]
    @pl.loop(0, G // 2 // unroll)
    def _(i):
        for u in range(unroll):
            pair(i * unroll + u)

def k1(nbr, ext, sel, corr, mask, unroll=1):
    return pl.pallas_call(
        functools.partial(k1_body, unroll),
        grid_spec=pltpu.PrefetchScalarGridSpec(
            num_scalar_prefetch=1, grid=(A // G,),
            in_specs=[pl.BlockSpec((9 * A, 256), lambda s, n: (0, 0)),
                      pl.BlockSpec((256, 2048), lambda s, n: (0, 0)),
                      pl.BlockSpec((G, 34560), lambda s, n: (s, 0)),
                      pl.BlockSpec((8, 16, 128), lambda s, n: (0, 0, 0))],
            out_specs=[pl.BlockSpec((PR, G, 128), lambda s, n: (0, s, 0)),
                       pl.BlockSpec((G // 2, PR, 768), lambda s, n: (s, 0, 0))],
            scratch_shapes=[pltpu.VMEM((9 * A, 16, 128), BF), pltpu.VMEM((288 * 16, 128), F32)]),
        out_shape=[jax.ShapeDtypeStruct((PR, A, 128), F32), jax.ShapeDtypeStruct((A // 2, PR, 768), BF)],
        compiler_params=pltpu.CompilerParams(vmem_limit_bytes=60 << 20, dimension_semantics=("arbitrary",)),
        name="descriptor",
    )(nbr, ext, sel, corr, mask)

def consts():
    i = jnp.arange(256)[:, None]; c = jnp.arange(2048)[None]
    sel = (((i >> 4) == (c >> 7)) & ((i & 15) == (c & 15))).astype(BF)
    k = jnp.arange(8)[:, None, None]; l = jnp.arange(128)[None, None]
    mask = jnp.broadcast_to(((l >> 4) == k), (8, 16, 128)).astype(BF)
    return sel, mask

def relay(corr):
    return corr.reshape(256, 34560)

PC = 16
def k2_body(d_ref, w1, b1, w2, b2, w3, b3, ro, e_ref, s_ref, acc, grad, rows):
    phase, c = pl.program_id(0), pl.program_id(1)
    last = pl.num_programs(1) - 1
    pad = jnp.zeros((128 - PR, H), BF)
    inside = c * (PC * NP) + lax.broadcasted_iota(jnp.int32, (PC * NP, H), 0) < NP * NP
    rows[:PC * NP, :] = jnp.where(inside, w1[...].astype(F32), 0.0)
    rows[PC * NP:, :] = jnp.zeros((8, H), F32)
    def weights(p):
        w = [rows[NP * v:NP * v + PR, :].astype(BF) for v in (p, p + 1)]
        return jnp.concatenate([w[0], pad, w[1], pad], 0)
    @pl.when(phase == 0)
    def _():
        t = jnp.zeros((A, H), F32)
        for p in range(0, PC, 2):
            x = jnp.concatenate([d_ref[p], d_ref[p + 1]], 1).astype(BF)
            t = t + dot(x, weights(p))
        acc[...] = jnp.where(c == 0, 0.0, acc[...]) + t
        @pl.when(c == last)
        def _():
            act1 = jnp.tanh(acc[...] + b1[...])
            th2 = jnp.tanh(dot(act1.astype(BF), w2[...]) + b2[...])
            act2 = act1 + th2
            th3 = jnp.tanh(dot(act2.astype(BF), w3[...]) + b3[...])
            e_ref[...] = jnp.sum((act2 + th3) * ro[...], axis=1, keepdims=True)
            g3 = (ro[...] * (1.0 - th3 * th3)).astype(BF)
            back2 = ro[...] + dot_nt(g3, w3[...])
            g2 = (back2 * (1.0 - th2 * th2)).astype(BF)
            back1 = back2 + dot_nt(g2, w2[...])
            grad[...] = (back1 * (1.0 - act1 * act1)).astype(BF)
    @pl.when(phase == 1)
    def _():
        for p in range(0, PC, 2):
            t = dot_nt(grad[...], weights(p))
            s_ref[p] = t[:, :128]
            s_ref[p + 1] = t[:, 128:]

def k2(d, w1, b1, w2, b2, w3, b3, ro):
    n = PR // PC
    row = lambda: pl.BlockSpec((1, H), lambda f, c: (0, 0))
    mat = lambda: pl.BlockSpec((H, H), lambda f, c: (0, 0))
    return pl.pallas_call(
        k2_body, grid=(2, n),
        in_specs=[pl.BlockSpec((PC, A, 128), lambda f, c: (jnp.where(f == 0, c, n - 1), 0, 0)),
                  pl.BlockSpec((PC * NP, H), lambda f, c: (c, 0)),
                  row(), mat(), row(), mat(), row(), row()],
        out_specs=[pl.BlockSpec((A, 1), lambda f, c: (0, 0)),
                   pl.BlockSpec((PC, A, 128), lambda f, c: (jnp.where(f == 0, 0, c), 0, 0))],
        scratch_shapes=[pltpu.VMEM((A, H), F32), pltpu.VMEM((A, H), BF), pltpu.VMEM((PC * NP + 8, H), F32)],
        out_shape=[jax.ShapeDtypeStruct((A, 1), F32), jax.ShapeDtypeStruct((PR, A, 128), F32)],
        compiler_params=pltpu.CompilerParams(vmem_limit_bytes=40 << 20),
        name="network",
    )(d, w1, b1, w2, b2, w3, b3, ro)

def k3_body(unroll, nbr, s_ref, o_ref, fold, out_ref, acc):
    step = pl.program_id(0)
    @pl.when(step == 0)
    def _():
        @pl.loop(0, 144)
        def _(c):
            acc[pl.ds(c * 16, 16)] = jnp.zeros((16, 16, 128), F32)
    s2 = s_ref.reshape(PR * G, 128)
    pad = jnp.zeros((128 - PR, 128), BF)
    lane = lax.broadcasted_iota(jnp.int32, (16, 128), 1) // 16
    def pair(i):
        st = [jnp.concatenate([s2[pl.ds(2 * i + h, PR, stride=G), :].astype(BF), pad], 0).T for h in range(2)]
        o = [[jnp.concatenate([o_ref[i, :, j * 256 + h * 128:j * 256 + h * 128 + 128], pad], 0) for j in range(3)] for h in range(2)]
        ot = jnp.concatenate([jnp.concatenate([o[0][j].T, o[1][j].T], 1) for j in range(3)], 0)
        lt = dot(ot, diag(*st)).astype(BF)
        for j in range(3):
            r = dot(lt[j * 128:(j + 1) * 128], diag(o[0][j], o[1][j]))
            for h in range(2):
                base = (step * G + 2 * i + h) * NK + 8 * j
                ns = [nbr[base + kk] for kk in range(8)]
                new = [acc[ns[kk]] + r[kk * 16:(kk + 1) * 16, h * 128:(h + 1) * 128] for kk in range(8)]
                for kk in range(8):
                    pltpu.store(acc.at[ns[kk]], new[kk], mask=lane == kk)
    @pl.loop(0, G // 2 // unroll)
    def _(i):
        for u in range(unroll):
            pair(i * unroll + u)
    @pl.when(step == pl.num_programs(0) - 1)
    def _():
        acc2 = acc.reshape(9 * A * 16, 128)
        @pl.loop(0, 9)
        def _(b):
            t = jnp.zeros((256, 256), F32)
            for q in range(0, 16, 2):
                x = jnp.concatenate([acc2[pl.ds(b * 4096 + q + h, 256, stride=16), :] for h in range(2)], 1).astype(BF)
                t = t + dot(x, fold[q * 128:(q + 2) * 128, :])
            out_ref[pl.ds(pl.multiple_of(b * 256, 256), 256), :] = t.astype(BF)

def k3(nbr, s, ot, fold, unroll=1):
    return pl.pallas_call(
        functools.partial(k3_body, unroll),
        grid_spec=pltpu.PrefetchScalarGridSpec(
            num_scalar_prefetch=1, grid=(A // G,),
            in_specs=[pl.BlockSpec((PR, G, 128), lambda s, n: (0, s, 0)),
                      pl.BlockSpec((G // 2, PR, 768), lambda s, n: (s, 0, 0)),
                      pl.BlockSpec((2048, 256), lambda s, n: (0, 0))],
            out_specs=pl.BlockSpec((9 * A, 256), lambda s, n: (0, 0)),
            scratch_shapes=[pltpu.VMEM((9 * A, 16, 128), F32)]),
        out_shape=jax.ShapeDtypeStruct((9 * A, 256), BF),
        compiler_params=pltpu.CompilerParams(vmem_limit_bytes=60 << 20),
        name="hamilton",
    )(nbr, s, ot, fold)

def fold_of():
    i = jnp.arange(2048)[:, None]; c = jnp.arange(256)[None]
    return (((i >> 7) == (c & 15)) & ((i & 15) == (c >> 4))).astype(BF)


MESH = pl.DeviceIdType.MESH


def greet(peers):
    barrier = pltpu.get_barrier_semaphore()
    for peer in peers:
        pl.semaphore_signal(barrier, inc=1, device_id=peer, device_id_type=MESH)
    pl.semaphore_wait(barrier, len(peers))


def push(src, dst, send, recv, peer):
    copy = pltpu.make_async_remote_copy(src_ref=src, dst_ref=dst, send_sem=send, recv_sem=recv,
                                        device_id=peer, device_id_type=MESH)
    copy.start()
    return copy


def halo_body(nx, ny, own, out, sy, ry, sx, rx):
    x, y = lax.axis_index("gx"), lax.axis_index("gy")
    onx = lambda k: {"gx": lax.rem(x + k + nx, nx)}
    ony = lambda k: {"gy": lax.rem(y + k + ny, ny)}
    greet([onx(1), onx(-1), ony(1), ony(-1)])
    out[1, 1] = own[...]
    first = [push(own, out.at[1, 1 - k], sy.at[(k + 1) // 2], ry.at[(k + 1) // 2], ony(k)) for k in (1, -1)]
    second = []
    def spread(j):
        for k in (1, -1):
            second.append(push(own if j == 1 else out.at[1, j], out.at[1 - k, j],
                               sx.at[(k + 1) // 2, j], rx.at[(k + 1) // 2, j], onx(k)))
    spread(1)
    for k, copy in zip((1, -1), first):
        copy.wait_recv()
        spread(1 - k)
    for copy in second:
        copy.wait_recv()
    for copy in first + second:
        copy.wait_send()


def halo(own, nx, ny):
    dma = pltpu.SemaphoreType.DMA
    return pl.pallas_call(
        functools.partial(halo_body, nx, ny),
        out_shape=jax.ShapeDtypeStruct((3, 3, A, 256), BF),
        in_specs=[pl.BlockSpec(memory_space=pltpu.VMEM)],
        out_specs=pl.BlockSpec(memory_space=pltpu.VMEM),
        scratch_shapes=[dma((2,)), dma((2,)), dma((2, 3)), dma((2, 3))],
        compiler_params=pltpu.CompilerParams(collective_id=0, has_side_effects=True),
        name="halo",
    )(own)


def exchange_body(nx, ny, part, pos, out, near, edge, far, chosen, sent, mid, s1, r1, s2, r2, s3, r3, s4, r4):
    x, y = lax.axis_index("gx"), lax.axis_index("gy")
    onx = lambda k: {"gx": lax.rem(x + k + nx, nx)}
    ony = lambda k: {"gy": lax.rem(y + k + ny, ny)}
    greet([onx(k) for k in range(1, nx)] + [ony(k) for k in range(1, ny)])
    first = {}
    for j in (0, 2, 1):
        for d, k in enumerate((1, -1)):
            first[d, j] = push(part.at[1 + k, j], near.at[d, j], s1.at[d, j], r1.at[d, j], onx(k))
    rows = nx * ny * 8
    r = lax.broadcasted_iota(jnp.int32, (rows, A), 0)
    hit = ((r >> 3) * 4 + (r & 3)) == pos[...]
    half = (r >> 2) & 1
    for h in range(2):
        chosen[:, h * A:(h + 1) * A] = jnp.where(hit & (half == h), 1.0, 0.0).astype(BF)

    def fold(j):
        first[0, j].wait_recv()
        first[1, j].wait_recv()
        return part[1, j].astype(F32) + near[0, j].astype(F32) + near[1, j].astype(F32)
    second = []
    for d, (j, k) in enumerate(((2, 1), (0, -1))):
        edge[d] = fold(j).astype(BF)
        second.append(push(edge.at[d], far.at[d], s2.at[d], r2.at[d], ony(k)))
    total = fold(1)
    for d in range(2):
        second[d].wait_recv()
        total = total + far[d].astype(F32)
    both = jnp.concatenate([total[:, :128], total[:, 128:]], 0).astype(BF)
    sent[...] = dot(chosen[...], both).reshape(nx, ny, 8, 128).astype(BF)
    third = [push(sent.at[lax.rem(x + k, nx)], mid.at[x], s3.at[k], r3.at[k], onx(k)) for k in range(1, nx)]
    mid[x] = sent[x]
    for copy in third:
        copy.wait_recv()
    fourth = [push(mid.at[:, lax.rem(y + k, ny)], out.at[:, y], s4.at[k], r4.at[k], ony(k)) for k in range(1, ny)]
    out[:, y] = mid[:, y]
    for copy in fourth:
        copy.wait_recv()
    for copy in list(first.values()) + second + third + fourth:
        copy.wait_send()


def exchange(part, position, nx, ny):
    dma = pltpu.SemaphoreType.DMA
    vmem = pl.BlockSpec(memory_space=pltpu.VMEM)
    return pl.pallas_call(
        functools.partial(exchange_body, nx, ny),
        out_shape=jax.ShapeDtypeStruct((nx, ny, 8, 128), BF),
        in_specs=[vmem, vmem], out_specs=vmem,
        scratch_shapes=[pltpu.VMEM((2, 3, A, 256), BF), pltpu.VMEM((2, A, 256), BF), pltpu.VMEM((2, A, 256), BF),
                        pltpu.VMEM((nx * ny * 8, 2 * A), BF), pltpu.VMEM((nx, ny, 8, 128), BF),
                        pltpu.VMEM((nx, ny, 8, 128), BF),
                        dma((2, 3)), dma((2, 3)), dma((2,)), dma((2,)), dma((nx,)), dma((nx,)), dma((ny,)), dma((ny,))],
        compiler_params=pltpu.CompilerParams(collective_id=1, has_side_effects=True, vmem_limit_bytes=40 << 20),
        name="exchange",
    )(part, position)


def on_device(density, neighbours, correlations, weight_first, bias_first, weight_second, bias_second,
              weight_third, bias_third, readout, destination):
    nx, ny = lax.axis_size("gx"), lax.axis_size("gy")
    sel, mask = consts()
    nbr = neighbours.reshape(A * NK)
    ext = halo(density.reshape(A, 256), nx, ny).reshape(9 * A, 256)
    row = lambda v: v.reshape(1, H)
    d, o = k1(nbr, ext, sel, relay(correlations), mask, 8)
    energy, slope = k2(d, weight_first, row(bias_first), weight_second, row(bias_second),
                       weight_third, row(bias_third), row(readout))
    part = k3(nbr, slope, o, fold_of(), 8).reshape(3, 3, A, 256)
    target = destination.reshape(A)
    order = jnp.arange(A, dtype=jnp.int32)
    earlier = (target[:, None] == target[None, :]) & (order[:, None] < order[None, :])
    position = target * 4 + jnp.sum(earlier.astype(jnp.int32), axis=0)
    received = exchange(part, position.reshape(1, A), nx, ny)
    blocks = received.reshape(nx * ny, 2, 4, 128).transpose(0, 2, 1, 3).reshape(1, nx * ny, 4, 256).astype(F32)
    return energy.reshape(1, 1, A), blocks


def solution(mesh):
    own = P("gx", "gy", None, None)
    return jax.shard_map(
        on_device,
        mesh=mesh,
        in_specs=(own, own, own, P(), P(), P(), P(), P(), P(), P(), own),
        out_specs=(P("gx", "gy", None), P(("gx", "gy"), None, None, None)),
        check_vma=False,
    )
```

```python
import functools
import numpy as np
import jax, jax.numpy as jnp
from jax import lax
from jax.experimental import pallas as pl
from jax.experimental.pallas import tpu as pltpu
from jax.sharding import PartitionSpec as P
F32, BF = jnp.float32, jnp.bfloat16
NP, NK, NO, H, A = 90, 24, 16, 256, 256
PR = 96
G = 16
NT = (((1,), (1,)), ((), ()))

def dot(a, b):
    return jnp.dot(a, b, preferred_element_type=F32)
def dot_nt(a, b):
    return lax.dot_general(a, b, NT, preferred_element_type=F32)

def diag(x, y):
    z = jnp.zeros_like(x)
    return jnp.concatenate([jnp.concatenate([x, z], 1), jnp.concatenate([z, y], 1)], 0)

def k1_body(unroll, nbr, ext, sel, corr, mask, w1_hbm, b1, w2, b2, w3, b3, ro, e_ref, s_hbm, o_ref,
            table, tmp, d_ref, w1, wide, rows, w_sem, s_sem):
    step = pl.program_id(0)
    fetch = pltpu.make_async_copy(w1_hbm, w1, w_sem)
    @pl.when(step == 0)
    def _():
        fetch.start()
        tmp[pl.ds(270 * 16, 18 * 16), :] = jnp.zeros((18 * 16, 128), F32)
        @pl.loop(0, 9)
        def _(b):
            own = ext[pl.ds(pl.multiple_of(b * 256, 256), 256), :]
            for o in range(0, 16, 2):
                t = dot(own, sel[:, o * 128:(o + 2) * 128])
                for h in range(2):
                    tmp[pl.ds(o + h, 256, stride=16), :] = t[:, h * 128:(h + 1) * 128]
            table[pl.ds(b * 256, 256)] = tmp[pl.ds(0, 4096), :].reshape(256, 16, 128).astype(BF)
    @pl.loop(0, 10)
    def _(c):
        for r in range(27):
            x = corr[:, pl.ds(pl.multiple_of((c * 27 + r) * 128, 128), 128)].astype(F32)
            tmp[pl.ds(pl.multiple_of((c * 27 + r) * 16, 16), 16), :] = x
    pad = jnp.zeros((128 - PR, 128), BF)
    d2 = d_ref.reshape(PR * A, 128)
    def bdiag(i, h, j):
        base = (step * G + 2 * i + h) * NK + 8 * j
        return jnp.concatenate([table[nbr[base + kk]] * mask[kk] for kk in range(8)], 0)
    def pair(i):
        o = [[tmp[pl.ds(j * 16 + 2 * i + h, PR, stride=48), :].astype(BF) for j in range(3)] for h in range(2)]
        ot = [[jnp.concatenate([o[h][j], pad], 0).T for j in range(3)] for h in range(2)]
        p = []
        for j in range(3):
            both = jnp.concatenate([o[0][j], o[1][j]], 1)
            o_ref[i, :, j * 256:(j + 1) * 256] = both
            p.append(dot(both, diag(bdiag(i, 0, j), bdiag(i, 1, j))).astype(BF))
        d = dot(jnp.concatenate(p, 1), jnp.concatenate([diag(ot[0][j], ot[1][j]) for j in range(3)], 0))
        for h in range(2):
            d2[pl.ds(step * G + 2 * i + h, PR, stride=A), :] = d[:, h * 128:(h + 1) * 128]
    @pl.loop(0, G // 2 // unroll)
    def _(i):
        for u in range(unroll):
            pair(i * unroll + u)
    @pl.when(step == pl.num_programs(0) - 1)
    def _():
        fetch.wait()
        gap = jnp.zeros((128 - PR, H), BF)
        t = jnp.zeros((A, H), F32)
        for c in range(PR // PC):
            n = min(PC * NP, NP * NP - c * PC * NP)
            rows[:n, :] = w1[c * PC * NP:c * PC * NP + n, :].astype(F32)
            rows[n:n + 8, :] = jnp.zeros((8, H), F32)
            for v in range(0, n // NP, 2):
                w = [rows[NP * u:NP * u + PR, :].astype(BF) for u in (v, v + 1)]
                w = jnp.concatenate([w[0], gap, w[1], gap], 0)
                p = c * PC + v
                wide[p // 2] = w
                t = t + dot(jnp.concatenate([d_ref[p], d_ref[p + 1]], 1).astype(BF), w)
        act1 = jnp.tanh(t + b1[...])
        th2 = jnp.tanh(dot(act1.astype(BF), w2[...]) + b2[...])
        act2 = act1 + th2
        th3 = jnp.tanh(dot(act2.astype(BF), w3[...]) + b3[...])
        e_ref[...] = jnp.sum(((act2 + th3) * ro[...]).T, axis=0, keepdims=True)
        g3 = (ro[...] * (1.0 - th3 * th3)).astype(BF)
        back2 = ro[...] + dot_nt(g3, w3[...])
        g2 = (back2 * (1.0 - th2 * th2)).astype(BF)
        back1 = back2 + dot_nt(g2, w2[...])
        g1 = (back1 * (1.0 - act1 * act1)).astype(BF)
        out = []
        for c in range(PR // PC):
            for p in range(c * PC, (c + 1) * PC, 2):
                if p < NP:
                    r = dot_nt(g1, wide[p // 2])
                    d_ref[p] = r[:, :128]
                    d_ref[p + 1] = r[:, 128:]
            here = pl.ds(c * PC, PC)
            out.append(pltpu.make_async_copy(d_ref.at[here], s_hbm.at[here], s_sem.at[c]))
            out[-1].start()
        for copy in out:
            copy.wait()

PC = 16
def k1(nbr, ext, sel, corr, mask, w1, b1, w2, b2, w3, b3, ro, unroll=8):
    row = lambda: pl.BlockSpec((1, H), lambda s, n: (0, 0))
    mat = lambda: pl.BlockSpec((H, H), lambda s, n: (0, 0))
    return pl.pallas_call(
        functools.partial(k1_body, unroll),
        grid_spec=pltpu.PrefetchScalarGridSpec(
            num_scalar_prefetch=1, grid=(A // G,),
            in_specs=[pl.BlockSpec((9 * A, 256), lambda s, n: (0, 0)),
                      pl.BlockSpec((256, 2048), lambda s, n: (0, 0)),
                      pl.BlockSpec((G, 34560), lambda s, n: (s, 0)),
                      pl.BlockSpec((8, 16, 128), lambda s, n: (0, 0, 0)),
                      pl.BlockSpec(memory_space=pl.ANY),
                      row(), mat(), row(), mat(), row(), row()],
            out_specs=[pl.BlockSpec((1, A), lambda s, n: (0, 0)),
                       pl.BlockSpec(memory_space=pl.ANY),
                       pl.BlockSpec((G // 2, PR, 768), lambda s, n: (s, 0, 0))],
            scratch_shapes=[pltpu.VMEM((9 * A, 16, 128), BF), pltpu.VMEM((288 * 16, 128), F32),
                            pltpu.VMEM((PR, A, 128), F32), pltpu.VMEM((NP * NP, H), BF),
                            pltpu.VMEM((NP // 2, 256, H), BF), pltpu.VMEM((PC * NP + 8, H), F32),
                            pltpu.SemaphoreType.DMA, pltpu.SemaphoreType.DMA((PR // PC,))]),
        out_shape=[jax.ShapeDtypeStruct((1, A), F32), jax.ShapeDtypeStruct((PR, A, 128), F32),
                   jax.ShapeDtypeStruct((A // 2, PR, 768), BF)],
        compiler_params=pltpu.CompilerParams(vmem_limit_bytes=60 << 20, dimension_semantics=("arbitrary",)),
        name="descriptor",
    )(nbr, ext, sel, corr, mask, w1, b1, w2, b2, w3, b3, ro)

def consts():
    i = np.arange(256)[:, None]; c = np.arange(2048)[None]
    sel = (((i >> 4) == (c >> 7)) & ((i & 15) == (c & 15))).astype(BF)
    k = jnp.arange(8)[:, None, None]; l = jnp.arange(128)[None, None]
    mask = jnp.broadcast_to(((l >> 4) == k), (8, 16, 128)).astype(BF)
    return jnp.asarray(sel), jnp.asarray(mask)

def relay(corr):
    return corr.reshape(256, 34560)

def k3_body(unroll, nbr, s_ref, o_ref, fold, out_ref, acc):
    step = pl.program_id(0)
    @pl.when(step == 0)
    def _():
        @pl.loop(0, 144)
        def _(c):
            acc[pl.ds(c * 16, 16)] = jnp.zeros((16, 16, 128), F32)
    s2 = s_ref.reshape(PR * G, 128)
    pad = jnp.zeros((128 - PR, 128), BF)
    lane = lax.broadcasted_iota(jnp.int32, (16, 128), 1) // 16
    def pair(i):
        st = [jnp.concatenate([s2[pl.ds(2 * i + h, PR, stride=G), :].astype(BF), pad], 0).T for h in range(2)]
        o = [[jnp.concatenate([o_ref[i, :, j * 256 + h * 128:j * 256 + h * 128 + 128], pad], 0) for j in range(3)] for h in range(2)]
        ot = jnp.concatenate([jnp.concatenate([o[0][j].T, o[1][j].T], 1) for j in range(3)], 0)
        lt = dot(ot, diag(*st)).astype(BF)
        for j in range(3):
            r = dot(lt[j * 128:(j + 1) * 128], diag(o[0][j], o[1][j]))
            for h in range(2):
                base = (step * G + 2 * i + h) * NK + 8 * j
                ns = [nbr[base + kk] for kk in range(8)]
                new = [acc[ns[kk]] + r[kk * 16:(kk + 1) * 16, h * 128:(h + 1) * 128] for kk in range(8)]
                for kk in range(8):
                    pltpu.store(acc.at[ns[kk]], new[kk], mask=lane == kk)
    @pl.loop(0, G // 2 // unroll)
    def _(i):
        for u in range(unroll):
            pair(i * unroll + u)
    @pl.when(step == pl.num_programs(0) - 1)
    def _():
        acc2 = acc.reshape(9 * A * 16, 128)
        @pl.loop(0, 9)
        def _(b):
            t = dot(jnp.concatenate([acc2[pl.ds(b * 4096 + q, 256, stride=16), :].astype(BF) for q in range(16)], 1), fold[...])
            out_ref[pl.ds(pl.multiple_of(b * 256, 256), 256), :] = t.astype(BF)

def k3(nbr, s, ot, fold, unroll=1):
    return pl.pallas_call(
        functools.partial(k3_body, unroll),
        grid_spec=pltpu.PrefetchScalarGridSpec(
            num_scalar_prefetch=1, grid=(A // G,),
            in_specs=[pl.BlockSpec((PR, G, 128), lambda s, n: (0, s, 0)),
                      pl.BlockSpec((G // 2, PR, 768), lambda s, n: (s, 0, 0)),
                      pl.BlockSpec((2048, 256), lambda s, n: (0, 0))],
            out_specs=pl.BlockSpec((9 * A, 256), lambda s, n: (0, 0)),
            scratch_shapes=[pltpu.VMEM((9 * A, 16, 128), F32)]),
        out_shape=jax.ShapeDtypeStruct((9 * A, 256), BF),
        compiler_params=pltpu.CompilerParams(vmem_limit_bytes=60 << 20),
        name="hamilton",
    )(nbr, s, ot, fold)

def fold_of():
    i = np.arange(2048)[:, None]; c = np.arange(256)[None]
    return jnp.asarray((((i >> 7) == (c & 15)) & ((i & 15) == (c >> 4))).astype(BF))


MESH = pl.DeviceIdType.MESH


def greet(peers):
    barrier = pltpu.get_barrier_semaphore()
    for peer in peers:
        pl.semaphore_signal(barrier, inc=1, device_id=peer, device_id_type=MESH)
    pl.semaphore_wait(barrier, len(peers))


def push(src, dst, send, recv, peer):
    copy = pltpu.make_async_remote_copy(src_ref=src, dst_ref=dst, send_sem=send, recv_sem=recv,
                                        device_id=peer, device_id_type=MESH)
    copy.start()
    return copy


def halo_body(nx, ny, own, out, sy, ry, sx, rx):
    x, y = lax.axis_index("gx"), lax.axis_index("gy")
    onx = lambda k: {"gx": lax.rem(x + k + nx, nx)}
    ony = lambda k: {"gy": lax.rem(y + k + ny, ny)}
    greet([onx(1), onx(-1), ony(1), ony(-1)])
    out[1, 1] = own[...]
    first = [push(own, out.at[1, 1 - k], sy.at[(k + 1) // 2], ry.at[(k + 1) // 2], ony(k)) for k in (1, -1)]
    second = []
    def spread(j):
        for k in (1, -1):
            second.append(push(own if j == 1 else out.at[1, j], out.at[1 - k, j],
                               sx.at[(k + 1) // 2, j], rx.at[(k + 1) // 2, j], onx(k)))
    spread(1)
    for k, copy in zip((1, -1), first):
        copy.wait_recv()
        spread(1 - k)
    for copy in second:
        copy.wait_recv()
    for copy in first + second:
        copy.wait_send()


def halo(own, nx, ny):
    dma = pltpu.SemaphoreType.DMA
    return pl.pallas_call(
        functools.partial(halo_body, nx, ny),
        out_shape=jax.ShapeDtypeStruct((3, 3, A, 256), BF),
        in_specs=[pl.BlockSpec(memory_space=pltpu.VMEM)],
        out_specs=pl.BlockSpec(memory_space=pltpu.VMEM),
        scratch_shapes=[dma((2,)), dma((2,)), dma((2, 3)), dma((2, 3))],
        compiler_params=pltpu.CompilerParams(collective_id=0, has_side_effects=True),
        name="halo",
    )(own)


def exchange_body(nx, ny, part, pos, out, mine, near, edge, far, chosen, sent, mid, sm, s1, r1, s2, r2, s3, r3, s4, r4):
    x, y = lax.axis_index("gx"), lax.axis_index("gy")
    onx = lambda k: {"gx": lax.rem(x + k + nx, nx)}
    ony = lambda k: {"gy": lax.rem(y + k + ny, ny)}
    take = pltpu.make_async_copy(part.at[1], mine, sm)
    take.start()
    greet([onx(k) for k in range(1, nx)] + [ony(k) for k in range(1, ny)])
    first = {}
    for j in (0, 2, 1):
        for d, k in enumerate((1, -1)):
            first[d, j] = push(part.at[1 + k, j], near.at[d, j], s1.at[d, j], r1.at[d, j], onx(k))
    rows = nx * ny * 8
    r = lax.broadcasted_iota(jnp.int32, (rows, A), 0)
    hit = ((r >> 3) * 4 + (r & 3)) == pos[...]
    half = (r >> 2) & 1
    for h in range(2):
        chosen[:, h * A:(h + 1) * A] = jnp.where(hit & (half == h), 1.0, 0.0).astype(BF)

    take.wait()

    def fold(j):
        first[0, j].wait_recv()
        first[1, j].wait_recv()
        return mine[j].astype(F32) + near[0, j].astype(F32) + near[1, j].astype(F32)
    second = []
    for d, (j, k) in enumerate(((2, 1), (0, -1))):
        edge[d] = fold(j).astype(BF)
        second.append(push(edge.at[d], far.at[d], s2.at[d], r2.at[d], ony(k)))
    total = fold(1)
    for d in range(2):
        second[d].wait_recv()
        total = total + far[d].astype(F32)
    both = jnp.concatenate([total[:, :128], total[:, 128:]], 0).astype(BF)
    sent[...] = dot(chosen[...], both).reshape(nx, ny, 8, 128).astype(BF)
    third = [push(sent.at[lax.rem(x + k, nx)], mid.at[x], s3.at[k], r3.at[k], onx(k)) for k in range(1, nx)]
    mid[x] = sent[x]
    for copy in third:
        copy.wait_recv()
    fourth = [push(mid.at[:, lax.rem(y + k, ny)], out.at[:, y], s4.at[k], r4.at[k], ony(k)) for k in range(1, ny)]
    out[:, y] = mid[:, y]
    for copy in fourth:
        copy.wait_recv()
    for copy in list(first.values()) + second + third + fourth:
        copy.wait_send()


def exchange(part, position, nx, ny):
    dma = pltpu.SemaphoreType.DMA
    vmem = pl.BlockSpec(memory_space=pltpu.VMEM)
    return pl.pallas_call(
        functools.partial(exchange_body, nx, ny),
        out_shape=jax.ShapeDtypeStruct((nx, ny, 8, 128), BF),
        in_specs=[pl.BlockSpec(memory_space=pl.ANY), vmem], out_specs=vmem,
        scratch_shapes=[pltpu.VMEM((3, A, 256), BF), pltpu.VMEM((2, 3, A, 256), BF), pltpu.VMEM((2, A, 256), BF), pltpu.VMEM((2, A, 256), BF),
                        pltpu.VMEM((nx * ny * 8, 2 * A), BF), pltpu.VMEM((nx, ny, 8, 128), BF),
                        pltpu.VMEM((nx, ny, 8, 128), BF),
                        dma, dma((2, 3)), dma((2, 3)), dma((2,)), dma((2,)), dma((nx,)), dma((nx,)), dma((ny,)), dma((ny,))],
        compiler_params=pltpu.CompilerParams(collective_id=1, has_side_effects=True, vmem_limit_bytes=40 << 20),
        name="exchange",
    )(part, position)


def on_device(density, neighbours, correlations, weight_first, bias_first, weight_second, bias_second,
              weight_third, bias_third, readout, destination):
    nx, ny = lax.axis_size("gx"), lax.axis_size("gy")
    sel, mask = consts()
    nbr = neighbours.reshape(A * NK)
    ext = halo(density.reshape(A, 256), nx, ny).reshape(9 * A, 256)
    row = lambda v: v.reshape(1, H)
    energy, slope, o = k1(nbr, ext, sel, relay(correlations), mask, weight_first, row(bias_first), weight_second,
                          row(bias_second), weight_third, row(bias_third), row(readout))
    part = k3(nbr, slope, o, fold_of(), 8).reshape(3, 3, A, 256)
    target = destination.reshape(A)
    order = jnp.arange(A, dtype=jnp.int32)
    earlier = (target[:, None] == target[None, :]) & (order[:, None] < order[None, :])
    position = target * 4 + jnp.sum(earlier.astype(jnp.int32), axis=0)
    received = exchange(part, position.reshape(1, A), nx, ny)
    blocks = received.reshape(nx * ny, 2, 4, 128).transpose(0, 2, 1, 3).reshape(1, nx * ny, 4, 256).astype(F32)
    return energy.reshape(1, 1, A), blocks


def solution(mesh):
    own = P("gx", "gy", None, None)
    return jax.shard_map(
        on_device,
        mesh=mesh,
        in_specs=(own, own, own, P(), P(), P(), P(), P(), P(), P(), own),
        out_specs=(P("gx", "gy", None), P(("gx", "gy"), None, None, None)),
        check_vma=False,
    )
```

```python
import functools
import numpy as np
import jax, jax.numpy as jnp
from jax import lax
from jax.experimental import pallas as pl
from jax.experimental.pallas import tpu as pltpu
from jax.sharding import PartitionSpec as P
F32, BF = jnp.float32, jnp.bfloat16
NP, NK, NO, H, A = 90, 24, 16, 256, 256
PR = 96
G = 16
NT = (((1,), (1,)), ((), ()))

def dot(a, b):
    return jnp.dot(a, b, preferred_element_type=F32)
def dot_nt(a, b):
    return lax.dot_general(a, b, NT, preferred_element_type=F32)

def diag(x, y):
    z = jnp.zeros_like(x)
    return jnp.concatenate([jnp.concatenate([x, z], 1), jnp.concatenate([z, y], 1)], 0)

def k1_body(unroll, nbr, ext, sel, o_ref, w1_hbm, b1, w2, b2, w3, b3, ro, e_ref, s_hbm,
            table, tmp, mask, d_ref, w1, wide, rows, w_sem, s_sem):
    step = pl.program_id(0)
    fetch = pltpu.make_async_copy(w1_hbm, w1, w_sem)
    @pl.when(step == 0)
    def _():
        fetch.start()
        lane = lax.broadcasted_iota(jnp.int32, (16, 128), 1) >> 4
        for kk in range(8):
            mask[kk] = jnp.where(lane == kk, 1.0, 0.0).astype(BF)
        @pl.loop(0, 9)
        def _(b):
            own = ext[pl.ds(pl.multiple_of(b * 256, 256), 256), :]
            for o in range(0, 16, 2):
                t = dot(own, sel[:, o * 128:(o + 2) * 128])
                for h in range(2):
                    tmp[pl.ds(o + h, 256, stride=16), :] = t[:, h * 128:(h + 1) * 128]
            table[pl.ds(b * 256, 256)] = tmp[pl.ds(0, 4096), :].reshape(256, 16, 128).astype(BF)
    pad = jnp.zeros((128 - PR, 128), BF)
    d2 = d_ref.reshape(PR * A, 128)
    def bdiag(i, h, j):
        return jnp.concatenate([table[nbr[step * G + 2 * i + h, 8 * j + kk]] * mask[kk] for kk in range(8)], 0)
    def pair(i):
        o = [[o_ref[i, :, j * 256 + h * 128:j * 256 + h * 128 + 128] for j in range(3)] for h in range(2)]
        ot = [[jnp.concatenate([o[h][j], pad], 0).T for j in range(3)] for h in range(2)]
        p = []
        for j in range(3):
            p.append(dot(o_ref[i, :, j * 256:(j + 1) * 256], diag(bdiag(i, 0, j), bdiag(i, 1, j))).astype(BF))
        d = dot(jnp.concatenate(p, 1), jnp.concatenate([diag(ot[0][j], ot[1][j]) for j in range(3)], 0))
        for h in range(2):
            d2[pl.ds(step * G + 2 * i + h, PR, stride=A), :] = d[:, h * 128:(h + 1) * 128]
    @pl.loop(0, G // 2 // unroll)
    def _(i):
        for u in range(unroll):
            pair(i * unroll + u)
    @pl.when(step == pl.num_programs(0) - 1)
    def _():
        fetch.wait()
        gap = jnp.zeros((128 - PR, H), BF)
        t = jnp.zeros((A, H), F32)
        for c in range(PR // PC):
            n = min(PC * NP, NP * NP - c * PC * NP)
            rows[:n, :] = w1[c * PC * NP:c * PC * NP + n, :].astype(F32)
            rows[n:n + 8, :] = jnp.zeros((8, H), F32)
            for v in range(0, n // NP, 2):
                w = [rows[NP * u:NP * u + PR, :].astype(BF) for u in (v, v + 1)]
                w = jnp.concatenate([w[0], gap, w[1], gap], 0)
                p = c * PC + v
                wide[p // 2] = w
                t = t + dot(jnp.concatenate([d_ref[p], d_ref[p + 1]], 1).astype(BF), w)
        act1 = jnp.tanh(t + b1[...])
        th2 = jnp.tanh(dot(act1.astype(BF), w2[...]) + b2[...])
        act2 = act1 + th2
        th3 = jnp.tanh(dot(act2.astype(BF), w3[...]) + b3[...])
        e_ref[...] = jnp.sum(((act2 + th3) * ro[...]).T, axis=0, keepdims=True)
        g3 = (ro[...] * (1.0 - th3 * th3)).astype(BF)
        back2 = ro[...] + dot_nt(g3, w3[...])
        g2 = (back2 * (1.0 - th2 * th2)).astype(BF)
        back1 = back2 + dot_nt(g2, w2[...])
        g1 = (back1 * (1.0 - act1 * act1)).astype(BF)
        out = []
        for c in range(PR // PC):
            for p in range(c * PC, (c + 1) * PC, 2):
                if p < NP:
                    r = dot_nt(g1, wide[p // 2])
                    d_ref[p] = r[:, :128]
                    d_ref[p + 1] = r[:, 128:]
            here = pl.ds(c * PC, PC)
            out.append(pltpu.make_async_copy(d_ref.at[here], s_hbm.at[here], s_sem.at[c]))
            out[-1].start()
        for copy in out:
            copy.wait()

PC = 16
def k1(nbr, ext, sel, o, w1, b1, w2, b2, w3, b3, ro, unroll=8):
    row = lambda: pl.BlockSpec((1, H), lambda s, n: (0, 0))
    mat = lambda: pl.BlockSpec((H, H), lambda s, n: (0, 0))
    return pl.pallas_call(
        functools.partial(k1_body, unroll),
        grid_spec=pltpu.PrefetchScalarGridSpec(
            num_scalar_prefetch=1, grid=(A // G,),
            in_specs=[pl.BlockSpec((9 * A, 256), lambda s, n: (0, 0)),
                      pl.BlockSpec((256, 2048), lambda s, n: (0, 0)),
                      pl.BlockSpec((G // 2, PR, 768), lambda s, n: (s, 0, 0)),
                      pl.BlockSpec(memory_space=pl.ANY),
                      row(), mat(), row(), mat(), row(), row()],
            out_specs=[pl.BlockSpec((1, A), lambda s, n: (0, 0)),
                       pl.BlockSpec(memory_space=pl.ANY)],
            scratch_shapes=[pltpu.VMEM((9 * A, 16, 128), BF), pltpu.VMEM((4096, 128), F32), pltpu.VMEM((8, 16, 128), BF),
                            pltpu.VMEM((PR, A, 128), F32), pltpu.VMEM((NP * NP, H), BF),
                            pltpu.VMEM((NP // 2, 256, H), BF), pltpu.VMEM((PC * NP + 8, H), F32),
                            pltpu.SemaphoreType.DMA, pltpu.SemaphoreType.DMA((PR // PC,))]),
        out_shape=[jax.ShapeDtypeStruct((1, A), F32), jax.ShapeDtypeStruct((PR, A, 128), F32)],
        compiler_params=pltpu.CompilerParams(vmem_limit_bytes=60 << 20, dimension_semantics=("arbitrary",)),
        name="descriptor",
    )(nbr, ext, sel, o, w1, b1, w2, b2, w3, b3, ro)

def consts():
    i = np.arange(256)[:, None]; c = np.arange(2048)[None]
    sel = (((i >> 4) == (c >> 7)) & ((i & 15) == (c & 15))).astype(BF)
    return jnp.asarray(sel)

def relay(corr):
    return corr.reshape(256, 34560)

def k3_body(unroll, nbr, s_ref, o_ref, fold, out_ref, acc):
    step = pl.program_id(0)
    @pl.when(step == 0)
    def _():
        @pl.loop(0, 144)
        def _(c):
            acc[pl.ds(c * 16, 16)] = jnp.zeros((16, 16, 128), F32)
    s2 = s_ref.reshape(PR * G, 128)
    pad = jnp.zeros((128 - PR, 128), BF)
    lane = lax.broadcasted_iota(jnp.int32, (16, 128), 1) // 16
    def pair(i):
        st = [jnp.concatenate([s2[pl.ds(2 * i + h, PR, stride=G), :].astype(BF), pad], 0).T for h in range(2)]
        o = [[jnp.concatenate([o_ref[i, :, j * 256 + h * 128:j * 256 + h * 128 + 128], pad], 0) for j in range(3)] for h in range(2)]
        ot = jnp.concatenate([jnp.concatenate([o[0][j].T, o[1][j].T], 1) for j in range(3)], 0)
        lt = dot(ot, diag(*st)).astype(BF)
        for j in range(3):
            r = dot(lt[j * 128:(j + 1) * 128], diag(o[0][j], o[1][j]))
            for h in range(2):
                ns = [nbr[step * G + 2 * i + h, 8 * j + kk] for kk in range(8)]
                new = [acc[ns[kk]] + r[kk * 16:(kk + 1) * 16, h * 128:(h + 1) * 128] for kk in range(8)]
                for kk in range(8):
                    pltpu.store(acc.at[ns[kk]], new[kk], mask=lane == kk)
    @pl.loop(0, G // 2 // unroll)
    def _(i):
        for u in range(unroll):
            pair(i * unroll + u)
    @pl.when(step == pl.num_programs(0) - 1)
    def _():
        acc2 = acc.reshape(9 * A * 16, 128)
        @pl.loop(0, 9)
        def _(b):
            t = dot(jnp.concatenate([acc2[pl.ds(b * 4096 + q, 256, stride=16), :].astype(BF) for q in range(16)], 1), fold[...])
            out_ref[pl.ds(pl.multiple_of(b * 256, 256), 256), :] = t.astype(BF)

def k3(nbr, s, ot, fold, unroll=1):
    return pl.pallas_call(
        functools.partial(k3_body, unroll),
        grid_spec=pltpu.PrefetchScalarGridSpec(
            num_scalar_prefetch=1, grid=(A // G,),
            in_specs=[pl.BlockSpec((PR, G, 128), lambda s, n: (0, s, 0)),
                      pl.BlockSpec((G // 2, PR, 768), lambda s, n: (s, 0, 0)),
                      pl.BlockSpec((2048, 256), lambda s, n: (0, 0))],
            out_specs=pl.BlockSpec((9 * A, 256), lambda s, n: (0, 0)),
            scratch_shapes=[pltpu.VMEM((9 * A, 16, 128), F32)]),
        out_shape=jax.ShapeDtypeStruct((9 * A, 256), BF),
        compiler_params=pltpu.CompilerParams(vmem_limit_bytes=60 << 20),
        name="hamilton",
    )(nbr, s, ot, fold)

def fold_of():
    i = np.arange(2048)[:, None]; c = np.arange(256)[None]
    return jnp.asarray((((i >> 7) == (c & 15)) & ((i & 15) == (c >> 4))).astype(BF))


MESH = pl.DeviceIdType.MESH


def greet(peers):
    barrier = pltpu.get_barrier_semaphore()
    for peer in peers:
        pl.semaphore_signal(barrier, inc=1, device_id=peer, device_id_type=MESH)
    pl.semaphore_wait(barrier, len(peers))


def push(src, dst, send, recv, peer):
    copy = pltpu.make_async_remote_copy(src_ref=src, dst_ref=dst, send_sem=send, recv_sem=recv,
                                        device_id=peer, device_id_type=MESH)
    copy.start()
    return copy


def halo_body(nx, ny, own, corr, out, o_ref, tmp, keep, sy, ry, sx, rx):
    step = pl.program_id(0)
    x, y = lax.axis_index("gx"), lax.axis_index("gy")
    onx = lambda k: {"gx": lax.rem(x + k + nx, nx)}
    ony = lambda k: {"gy": lax.rem(y + k + ny, ny)}
    local = pltpu.make_async_copy(own, out.at[1, 1], keep)
    sends = lambda src, dst, *where: pltpu.make_async_remote_copy(
        src_ref=src, dst_ref=dst, send_sem=where[0], recv_sem=where[1], device_id=where[2], device_id_type=MESH)
    first = [sends(own, out.at[1, 1 - k], sy.at[(k + 1) // 2], ry.at[(k + 1) // 2], ony(k)) for k in (1, -1)]
    spread = [[sends(own if j == 1 else out.at[1, j], out.at[1 - k, j], sx.at[(k + 1) // 2, j], rx.at[(k + 1) // 2, j], onx(k))
               for k in (1, -1)] for j in range(3)]
    @pl.when(step == 0)
    def _():
        tmp[pl.ds(270 * 16, 18 * 16), :] = jnp.zeros((18 * 16, 128), F32)
        local.start()
        greet([onx(1), onx(-1), ony(1), ony(-1)])
        for copy in first + spread[1]:
            copy.start()
    @pl.when(step == 5)
    def _():
        for k, copy in zip((1, -1), first):
            copy.wait_recv()
            for c in spread[1 - k]:
                c.start()
    @pl.loop(0, 30)
    def _(c):
        for r in range(9):
            v = corr[:, pl.ds(pl.multiple_of((c * 9 + r) * 128, 128), 128)].astype(F32)
            tmp[pl.ds(pl.multiple_of((c * 9 + r) * 16, 16), 16), :] = v
    @pl.loop(0, G // 4)
    def _(i):
        for u in range(2):
            for j in range(3):
                for h in range(2):
                    v = tmp[pl.ds(j * 16 + 4 * i + 2 * u + h, PR, stride=48), :].astype(BF)
                    o_ref[2 * i + u, :, j * 256 + h * 128:j * 256 + h * 128 + 128] = v
    @pl.when(step == pl.num_programs(0) - 1)
    def _():
        local.wait()
        for group in spread:
            for copy in group:
                copy.wait_recv()
        for copy in first + spread[0] + spread[1] + spread[2]:
            copy.wait_send()


def halo(own, corr, nx, ny):
    dma = pltpu.SemaphoreType.DMA
    hbm = pl.BlockSpec(memory_space=pltpu.HBM)
    return pl.pallas_call(
        functools.partial(halo_body, nx, ny),
        grid=(A // G,),
        out_shape=[jax.ShapeDtypeStruct((3, 3, A, 256), BF), jax.ShapeDtypeStruct((A // 2, PR, 768), BF)],
        in_specs=[hbm, pl.BlockSpec((G, 34560), lambda s: (s, 0))],
        out_specs=[hbm, pl.BlockSpec((G // 2, PR, 768), lambda s: (s, 0, 0))],
        scratch_shapes=[pltpu.VMEM((288 * 16, 128), F32), dma, dma((2,)), dma((2,)), dma((2, 3)), dma((2, 3))],
        compiler_params=pltpu.CompilerParams(collective_id=0, has_side_effects=True, vmem_limit_bytes=40 << 20),
        name="halo",
    )(own, corr)


def exchange_body(nx, ny, part, pos, out, mine, near, edge, far, chosen, sent, mid, sm, s1, r1, s2, r2, s3, r3, s4, r4):
    x, y = lax.axis_index("gx"), lax.axis_index("gy")
    onx = lambda k: {"gx": lax.rem(x + k + nx, nx)}
    ony = lambda k: {"gy": lax.rem(y + k + ny, ny)}
    take = pltpu.make_async_copy(part.at[1], mine, sm)
    take.start()
    greet([onx(k) for k in range(1, nx)] + [ony(k) for k in range(1, ny)])
    first = {}
    for j in (0, 2, 1):
        for d, k in enumerate((1, -1)):
            first[d, j] = push(part.at[1 + k, j], near.at[d, j], s1.at[d, j], r1.at[d, j], onx(k))
    rows = nx * ny * 8
    r = lax.broadcasted_iota(jnp.int32, (rows, A), 0)
    hit = ((r >> 3) * 4 + (r & 3)) == pos[...]
    half = (r >> 2) & 1
    for h in range(2):
        chosen[:, h * A:(h + 1) * A] = jnp.where(hit & (half == h), 1.0, 0.0).astype(BF)

    take.wait()

    def fold(j):
        first[0, j].wait_recv()
        first[1, j].wait_recv()
        return mine[j].astype(F32) + near[0, j].astype(F32) + near[1, j].astype(F32)
    second = []
    for d, (j, k) in enumerate(((2, 1), (0, -1))):
        edge[d] = fold(j).astype(BF)
        second.append(push(edge.at[d], far.at[d], s2.at[d], r2.at[d], ony(k)))
    total = fold(1)
    for d in range(2):
        second[d].wait_recv()
        total = total + far[d].astype(F32)
    both = jnp.concatenate([total[:, :128], total[:, 128:]], 0).astype(BF)
    sent[...] = dot(chosen[...], both).reshape(nx, ny, 8, 128).astype(BF)
    third = [push(sent.at[lax.rem(x + k, nx)], mid.at[x], s3.at[k], r3.at[k], onx(k)) for k in range(1, nx)]
    mid[x] = sent[x]
    for copy in third:
        copy.wait_recv()
    fourth = [push(mid.at[:, lax.rem(y + k, ny)], out.at[:, y], s4.at[k], r4.at[k], ony(k)) for k in range(1, ny)]
    out[:, y] = mid[:, y]
    for copy in fourth:
        copy.wait_recv()
    for copy in list(first.values()) + second + third + fourth:
        copy.wait_send()


def exchange(part, position, nx, ny):
    dma = pltpu.SemaphoreType.DMA
    vmem = pl.BlockSpec(memory_space=pltpu.VMEM)
    return pl.pallas_call(
        functools.partial(exchange_body, nx, ny),
        out_shape=jax.ShapeDtypeStruct((nx, ny, 8, 128), BF),
        in_specs=[pl.BlockSpec(memory_space=pltpu.HBM), vmem], out_specs=vmem,
        scratch_shapes=[pltpu.VMEM((3, A, 256), BF), pltpu.VMEM((2, 3, A, 256), BF), pltpu.VMEM((2, A, 256), BF), pltpu.VMEM((2, A, 256), BF),
                        pltpu.VMEM((nx * ny * 8, 2 * A), BF), pltpu.VMEM((nx, ny, 8, 128), BF),
                        pltpu.VMEM((nx, ny, 8, 128), BF),
                        dma, dma((2, 3)), dma((2, 3)), dma((2,)), dma((2,)), dma((nx,)), dma((nx,)), dma((ny,)), dma((ny,))],
        compiler_params=pltpu.CompilerParams(collective_id=1, has_side_effects=True, vmem_limit_bytes=40 << 20),
        name="exchange",
    )(part, position)


def on_device(density, neighbours, correlations, weight_first, bias_first, weight_second, bias_second,
              weight_third, bias_third, readout, destination):
    nx, ny = lax.axis_size("gx"), lax.axis_size("gy")
    nbr = neighbours.reshape(A, NK)
    ext, o = halo(density.reshape(A, 256), relay(correlations), nx, ny)
    row = lambda v: v.reshape(1, H)
    energy, slope = k1(nbr, ext.reshape(9 * A, 256), consts(), o, weight_first, row(bias_first), weight_second,
                          row(bias_second), weight_third, row(bias_third), row(readout))
    part = k3(nbr, slope, o, fold_of(), 8).reshape(3, 3, A, 256)
    target = destination.reshape(A)
    order = jnp.arange(A, dtype=jnp.int32)
    earlier = (target[:, None] == target[None, :]) & (order[:, None] < order[None, :])
    position = target * 4 + jnp.sum(earlier.astype(jnp.int32), axis=0)
    received = exchange(part, position.reshape(1, A), nx, ny)
    blocks = received.reshape(nx * ny, 2, 4, 128).transpose(0, 2, 1, 3).reshape(1, nx * ny, 4, 256).astype(F32)
    return energy.reshape(1, 1, A), blocks


def solution(mesh):
    own = P("gx", "gy", None, None)
    return jax.shard_map(
        on_device,
        mesh=mesh,
        in_specs=(own, own, own, P(), P(), P(), P(), P(), P(), P(), own),
        out_specs=(P("gx", "gy", None), P(("gx", "gy"), None, None, None)),
        check_vma=False,
    )
```

```python
import functools
import numpy as np
import jax, jax.numpy as jnp
from jax import lax
from jax.experimental import pallas as pl
from jax.experimental.pallas import tpu as pltpu
from jax.sharding import PartitionSpec as P
F32, BF = jnp.float32, jnp.bfloat16
NP, NK, NO, H, A = 90, 24, 16, 256, 256
PR = 96
G = 16
NT = (((1,), (1,)), ((), ()))

def dot(a, b):
    return jnp.dot(a, b, preferred_element_type=F32)
def dot_nt(a, b):
    return lax.dot_general(a, b, NT, preferred_element_type=F32)

def diag(x, y):
    z = jnp.zeros_like(x)
    return jnp.concatenate([jnp.concatenate([x, z], 1), jnp.concatenate([z, y], 1)], 0)

def k1_body(unroll, nbr, ext, sel, o0, o1, o2, w1_hbm, b1, w2, b2, w3, b3, ro, e_ref, s_hbm,
            table, tmp, mask, d_ref, w1, wide, rows, w_sem, s_sem):
    step = pl.program_id(0)
    fetch = pltpu.make_async_copy(w1_hbm, w1, w_sem)
    @pl.when(step == 0)
    def _():
        fetch.start()
        lane = lax.broadcasted_iota(jnp.int32, (16, 128), 1) >> 4
        for kk in range(8):
            mask[kk] = jnp.where(lane == kk, 1.0, 0.0).astype(BF)
        @pl.loop(0, 9)
        def _(b):
            own = ext[pl.ds(pl.multiple_of(b * 256, 256), 256), :]
            for o in range(0, 16, 2):
                t = dot(own, sel[:, o * 128:(o + 2) * 128])
                for h in range(2):
                    tmp[pl.ds(o + h, 256, stride=16), :] = t[:, h * 128:(h + 1) * 128]
            table[pl.ds(b * 256, 256)] = tmp[pl.ds(0, 4096), :].reshape(256, 16, 128).astype(BF)
    pad = jnp.zeros((128 - PR, 128), BF)
    d2 = d_ref.reshape(PR * A, 128)
    def bdiag(i, h, j):
        return jnp.concatenate([table[nbr[step * G + 2 * i + h, 8 * j + kk]] * mask[kk] for kk in range(8)], 0)
    def pair(i):
        o = [[v[i, :, h * 128:h * 128 + 128] for v in (o0, o1, o2)] for h in range(2)]
        ot = [[jnp.concatenate([o[h][j], pad], 0).T for j in range(3)] for h in range(2)]
        p = []
        for j in range(3):
            p.append(dot((o0, o1, o2)[j][i], diag(bdiag(i, 0, j), bdiag(i, 1, j))).astype(BF))
        d = dot(jnp.concatenate(p, 1), jnp.concatenate([diag(ot[0][j], ot[1][j]) for j in range(3)], 0))
        for h in range(2):
            d2[pl.ds(step * G + 2 * i + h, PR, stride=A), :] = d[:, h * 128:(h + 1) * 128]
    @pl.loop(0, G // 2 // unroll)
    def _(i):
        for u in range(unroll):
            pair(i * unroll + u)
    @pl.when(step == pl.num_programs(0) - 1)
    def _():
        fetch.wait()
        gap = jnp.zeros((128 - PR, H), BF)
        t = jnp.zeros((A, H), F32)
        for c in range(PR // PC):
            n = min(PC * NP, NP * NP - c * PC * NP)
            rows[:n, :] = w1[c * PC * NP:c * PC * NP + n, :].astype(F32)
            rows[n:n + 8, :] = jnp.zeros((8, H), F32)
            for v in range(0, n // NP, 2):
                w = [rows[NP * u:NP * u + PR, :].astype(BF) for u in (v, v + 1)]
                w = jnp.concatenate([w[0], gap, w[1], gap], 0)
                p = c * PC + v
                wide[p // 2] = w
                t = t + dot(jnp.concatenate([d_ref[p], d_ref[p + 1]], 1).astype(BF), w)
        act1 = jnp.tanh(t + b1[...])
        th2 = jnp.tanh(dot(act1.astype(BF), w2[...]) + b2[...])
        act2 = act1 + th2
        th3 = jnp.tanh(dot(act2.astype(BF), w3[...]) + b3[...])
        e_ref[...] = jnp.sum(((act2 + th3) * ro[...]).T, axis=0, keepdims=True)
        g3 = (ro[...] * (1.0 - th3 * th3)).astype(BF)
        back2 = ro[...] + dot_nt(g3, w3[...])
        g2 = (back2 * (1.0 - th2 * th2)).astype(BF)
        back1 = back2 + dot_nt(g2, w2[...])
        g1 = (back1 * (1.0 - act1 * act1)).astype(BF)
        out = []
        for c in range(PR // PC):
            for p in range(c * PC, (c + 1) * PC, 2):
                if p < NP:
                    r = dot_nt(g1, wide[p // 2])
                    d_ref[p] = r[:, :128]
                    d_ref[p + 1] = r[:, 128:]
            here = pl.ds(c * PC, PC)
            out.append(pltpu.make_async_copy(d_ref.at[here], s_hbm.at[here], s_sem.at[c]))
            out[-1].start()
        for copy in out:
            copy.wait()

PC = 16
def k1(nbr, ext, sel, o, w1, b1, w2, b2, w3, b3, ro, unroll=8):
    row = lambda: pl.BlockSpec((1, H), lambda s, n: (0, 0))
    mat = lambda: pl.BlockSpec((H, H), lambda s, n: (0, 0))
    return pl.pallas_call(
        functools.partial(k1_body, unroll),
        grid_spec=pltpu.PrefetchScalarGridSpec(
            num_scalar_prefetch=1, grid=(A // G,),
            in_specs=[pl.BlockSpec((9 * A, 256), lambda s, n: (0, 0)),
                      pl.BlockSpec((256, 2048), lambda s, n: (0, 0)),
                      *[pl.BlockSpec((G // 2, PR, 256), lambda s, n: (s, 0, 0))] * 3,
                      pl.BlockSpec(memory_space=pl.ANY),
                      row(), mat(), row(), mat(), row(), row()],
            out_specs=[pl.BlockSpec((1, A), lambda s, n: (0, 0)),
                       pl.BlockSpec(memory_space=pl.ANY)],
            scratch_shapes=[pltpu.VMEM((9 * A, 16, 128), BF), pltpu.VMEM((4096, 128), F32), pltpu.VMEM((8, 16, 128), BF),
                            pltpu.VMEM((PR, A, 128), F32), pltpu.VMEM((NP * NP, H), BF),
                            pltpu.VMEM((NP // 2, 256, H), BF), pltpu.VMEM((PC * NP + 8, H), F32),
                            pltpu.SemaphoreType.DMA, pltpu.SemaphoreType.DMA((PR // PC,))]),
        out_shape=[jax.ShapeDtypeStruct((1, A), F32), jax.ShapeDtypeStruct((PR, A, 128), F32)],
        compiler_params=pltpu.CompilerParams(vmem_limit_bytes=60 << 20, dimension_semantics=("arbitrary",)),
        name="descriptor",
    )(nbr, ext, sel, *o, w1, b1, w2, b2, w3, b3, ro)

def consts():
    i = np.arange(256)[:, None]; c = np.arange(2048)[None]
    sel = (((i >> 4) == (c >> 7)) & ((i & 15) == (c & 15))).astype(BF)
    return jnp.asarray(sel)

def relay(corr):
    return corr.reshape(256, 34560)

def k3_body(unroll, nbr, s0, s1, s2, o0, o1, o2, fold, out_ref, acc):
    step = pl.program_id(0)
    @pl.when(step == 0)
    def _():
        @pl.loop(0, 144)
        def _(c):
            acc[pl.ds(c * 16, 16)] = jnp.zeros((16, 16, 128), F32)
    slopes = [v.reshape(PR // 3 * G, 128) for v in (s0, s1, s2)]
    pad = jnp.zeros((128 - PR, 128), BF)
    lane = lax.broadcasted_iota(jnp.int32, (16, 128), 1) // 16
    def pair(i):
        st = [jnp.concatenate([v[pl.ds(2 * i + h, PR // 3, stride=G), :].astype(BF) for v in slopes] + [pad], 0).T for h in range(2)]
        o = [[jnp.concatenate([v[i, :, h * 128:h * 128 + 128], pad], 0) for v in (o0, o1, o2)] for h in range(2)]
        ot = jnp.concatenate([jnp.concatenate([o[0][j].T, o[1][j].T], 1) for j in range(3)], 0)
        lt = dot(ot, diag(*st)).astype(BF)
        for j in range(3):
            r = dot(lt[j * 128:(j + 1) * 128], diag(o[0][j], o[1][j]))
            for h in range(2):
                ns = [nbr[step * G + 2 * i + h, 8 * j + kk] for kk in range(8)]
                new = [acc[ns[kk]] + r[kk * 16:(kk + 1) * 16, h * 128:(h + 1) * 128] for kk in range(8)]
                for kk in range(8):
                    pltpu.store(acc.at[ns[kk]], new[kk], mask=lane == kk)
    @pl.loop(0, G // 2 // unroll)
    def _(i):
        for u in range(unroll):
            pair(i * unroll + u)
    @pl.when(step == pl.num_programs(0) - 1)
    def _():
        acc2 = acc.reshape(9 * A * 16, 128)
        @pl.loop(0, 9)
        def _(b):
            t = dot(jnp.concatenate([acc2[pl.ds(b * 4096 + q, 256, stride=16), :].astype(BF) for q in range(16)], 1), fold[...])
            out_ref[pl.ds(pl.multiple_of(b * 256, 256), 256), :] = t.astype(BF)

def k3(nbr, s, ot, fold, unroll=1):
    return pl.pallas_call(
        functools.partial(k3_body, unroll),
        grid_spec=pltpu.PrefetchScalarGridSpec(
            num_scalar_prefetch=1, grid=(A // G,),
            in_specs=[*[pl.BlockSpec((PR // 3, G, 128), functools.partial(lambda c, s, n: (c, s, 0), c)) for c in range(3)],
                      *[pl.BlockSpec((G // 2, PR, 256), lambda s, n: (s, 0, 0))] * 3,
                      pl.BlockSpec((2048, 256), lambda s, n: (0, 0))],
            out_specs=pl.BlockSpec((9 * A, 256), lambda s, n: (0, 0)),
            scratch_shapes=[pltpu.VMEM((9 * A, 16, 128), F32)]),
        out_shape=jax.ShapeDtypeStruct((9 * A, 256), BF),
        compiler_params=pltpu.CompilerParams(vmem_limit_bytes=60 << 20),
        name="hamilton",
    )(nbr, s, s, s, *ot, fold)

def fold_of():
    i = np.arange(2048)[:, None]; c = np.arange(256)[None]
    return jnp.asarray((((i >> 7) == (c & 15)) & ((i & 15) == (c >> 4))).astype(BF))


MESH = pl.DeviceIdType.MESH


def greet(peers):
    barrier = pltpu.get_barrier_semaphore()
    for peer in peers:
        pl.semaphore_signal(barrier, inc=1, device_id=peer, device_id_type=MESH)
    pl.semaphore_wait(barrier, len(peers))


def push(src, dst, send, recv, peer):
    copy = pltpu.make_async_remote_copy(src_ref=src, dst_ref=dst, send_sem=send, recv_sem=recv,
                                        device_id=peer, device_id_type=MESH)
    copy.start()
    return copy


def halo_body(nx, ny, own, c0, c1, c2, out, o0, o1, o2, tmp, keep, sy, ry, sx, rx):
    step = pl.program_id(0)
    x, y = lax.axis_index("gx"), lax.axis_index("gy")
    onx = lambda k: {"gx": lax.rem(x + k + nx, nx)}
    ony = lambda k: {"gy": lax.rem(y + k + ny, ny)}
    local = pltpu.make_async_copy(own, out.at[1, 1], keep)
    sends = lambda src, dst, *where: pltpu.make_async_remote_copy(
        src_ref=src, dst_ref=dst, send_sem=where[0], recv_sem=where[1], device_id=where[2], device_id_type=MESH)
    first = [sends(own, out.at[1, 1 - k], sy.at[(k + 1) // 2], ry.at[(k + 1) // 2], ony(k)) for k in (1, -1)]
    spread = [[sends(own if j == 1 else out.at[1, j], out.at[1 - k, j], sx.at[(k + 1) // 2, j], rx.at[(k + 1) // 2, j], onx(k))
               for k in (1, -1)] for j in range(3)]
    @pl.when(step == 0)
    def _():
        tmp[pl.ds(270 * 16, 18 * 16), :] = jnp.zeros((18 * 16, 128), F32)
        local.start()
        greet([onx(1), onx(-1), ony(1), ony(-1)])
        for copy in first + spread[1]:
            copy.start()
    @pl.when(step == 5)
    def _():
        for k, copy in zip((1, -1), first):
            copy.wait_recv()
            for c in spread[1 - k]:
                c.start()
    for part, corr in enumerate((c0, c1, c2)):
        @pl.loop(0, 10)
        def _(c):
            for r in range(9):
                v = corr[:, pl.ds(pl.multiple_of((c * 9 + r) * 128, 128), 128)].astype(F32)
                tmp[pl.ds(pl.multiple_of((part * 90 + c * 9 + r) * 16, 16), 16), :] = v
    @pl.loop(0, G // 4)
    def _(i):
        for u in range(2):
            for j in range(3):
                for h in range(2):
                    v = tmp[pl.ds(j * 16 + 4 * i + 2 * u + h, PR, stride=48), :].astype(BF)
                    (o0, o1, o2)[j][2 * i + u, :, h * 128:h * 128 + 128] = v
    @pl.when(step == pl.num_programs(0) - 1)
    def _():
        local.wait()
        for group in spread:
            for copy in group:
                copy.wait_recv()
        for copy in first + spread[0] + spread[1] + spread[2]:
            copy.wait_send()


def halo(own, corr, nx, ny):
    dma = pltpu.SemaphoreType.DMA
    hbm = pl.BlockSpec(memory_space=pltpu.HBM)
    return pl.pallas_call(
        functools.partial(halo_body, nx, ny),
        grid=(A // G,),
        out_shape=[jax.ShapeDtypeStruct((3, 3, A, 256), BF), *[jax.ShapeDtypeStruct((A // 2, PR, 256), BF)] * 3],
        in_specs=[hbm, *[pl.BlockSpec((G, 11520), functools.partial(lambda c, s: (s, c), c)) for c in range(3)]],
        out_specs=[hbm, *[pl.BlockSpec((G // 2, PR, 256), lambda s: (s, 0, 0))] * 3],
        scratch_shapes=[pltpu.VMEM((288 * 16, 128), F32), dma, dma((2,)), dma((2,)), dma((2, 3)), dma((2, 3))],
        compiler_params=pltpu.CompilerParams(collective_id=0, has_side_effects=True, vmem_limit_bytes=40 << 20),
        name="halo",
    )(own, corr, corr, corr)


def exchange_body(nx, ny, part, pos, out, mine, near, edge, far, chosen, sent, mid, sm, s1, r1, s2, r2, s3, r3, s4, r4):
    x, y = lax.axis_index("gx"), lax.axis_index("gy")
    onx = lambda k: {"gx": lax.rem(x + k + nx, nx)}
    ony = lambda k: {"gy": lax.rem(y + k + ny, ny)}
    take = pltpu.make_async_copy(part.at[1], mine, sm)
    take.start()
    greet([onx(k) for k in range(1, nx)] + [ony(k) for k in range(1, ny)])
    first = {}
    for j in (0, 2, 1):
        for d, k in enumerate((1, -1)):
            first[d, j] = push(part.at[1 + k, j], near.at[d, j], s1.at[d, j], r1.at[d, j], onx(k))
    rows = nx * ny * 8
    r = lax.broadcasted_iota(jnp.int32, (rows, A), 0)
    hit = ((r >> 3) * 4 + (r & 3)) == pos[...]
    half = (r >> 2) & 1
    for h in range(2):
        chosen[:, h * A:(h + 1) * A] = jnp.where(hit & (half == h), 1.0, 0.0).astype(BF)

    take.wait()

    def fold(j):
        first[0, j].wait_recv()
        first[1, j].wait_recv()
        return mine[j].astype(F32) + near[0, j].astype(F32) + near[1, j].astype(F32)
    second = []
    for d, (j, k) in enumerate(((2, 1), (0, -1))):
        edge[d] = fold(j).astype(BF)
        second.append(push(edge.at[d], far.at[d], s2.at[d], r2.at[d], ony(k)))
    total = fold(1)
    for d in range(2):
        second[d].wait_recv()
        total = total + far[d].astype(F32)
    both = jnp.concatenate([total[:, :128], total[:, 128:]], 0).astype(BF)
    sent[...] = dot(chosen[...], both).reshape(nx, ny, 8, 128).astype(BF)
    third = [push(sent.at[lax.rem(x + k, nx)], mid.at[x], s3.at[k], r3.at[k], onx(k)) for k in range(1, nx)]
    mid[x] = sent[x]
    for copy in third:
        copy.wait_recv()
    fourth = [push(mid.at[:, lax.rem(y + k, ny)], out.at[:, y], s4.at[k], r4.at[k], ony(k)) for k in range(1, ny)]
    out[:, y] = mid[:, y]
    for copy in fourth:
        copy.wait_recv()
    for copy in list(first.values()) + second + third + fourth:
        copy.wait_send()


def exchange(part, position, nx, ny):
    dma = pltpu.SemaphoreType.DMA
    vmem = pl.BlockSpec(memory_space=pltpu.VMEM)
    return pl.pallas_call(
        functools.partial(exchange_body, nx, ny),
        out_shape=jax.ShapeDtypeStruct((nx, ny, 8, 128), BF),
        in_specs=[pl.BlockSpec(memory_space=pltpu.HBM), vmem], out_specs=vmem,
        scratch_shapes=[pltpu.VMEM((3, A, 256), BF), pltpu.VMEM((2, 3, A, 256), BF), pltpu.VMEM((2, A, 256), BF), pltpu.VMEM((2, A, 256), BF),
                        pltpu.VMEM((nx * ny * 8, 2 * A), BF), pltpu.VMEM((nx, ny, 8, 128), BF),
                        pltpu.VMEM((nx, ny, 8, 128), BF),
                        dma, dma((2, 3)), dma((2, 3)), dma((2,)), dma((2,)), dma((nx,)), dma((nx,)), dma((ny,)), dma((ny,))],
        compiler_params=pltpu.CompilerParams(collective_id=1, has_side_effects=True, vmem_limit_bytes=40 << 20),
        name="exchange",
    )(part, position)


def on_device(density, neighbours, correlations, weight_first, bias_first, weight_second, bias_second,
              weight_third, bias_third, readout, destination):
    nx, ny = lax.axis_size("gx"), lax.axis_size("gy")
    nbr = neighbours.reshape(A, NK)
    ext, *o = halo(density.reshape(A, 256), relay(correlations), nx, ny)
    row = lambda v: v.reshape(1, H)
    energy, slope = k1(nbr, ext.reshape(9 * A, 256), consts(), o, weight_first, row(bias_first), weight_second,
                          row(bias_second), weight_third, row(bias_third), row(readout))
    part = k3(nbr, slope, o, fold_of(), 8).reshape(3, 3, A, 256)
    target = destination.reshape(A)
    order = jnp.arange(A, dtype=jnp.int32)
    earlier = (target[:, None] == target[None, :]) & (order[:, None] < order[None, :])
    position = target * 4 + jnp.sum(earlier.astype(jnp.int32), axis=0)
    received = exchange(part, position.reshape(1, A), nx, ny)
    blocks = received.reshape(nx * ny, 2, 4, 128).transpose(0, 2, 1, 3).reshape(1, nx * ny, 4, 256).astype(F32)
    return energy.reshape(1, 1, A), blocks


def solution(mesh):
    own = P("gx", "gy", None, None)
    return jax.shard_map(
        on_device,
        mesh=mesh,
        in_specs=(own, own, own, P(), P(), P(), P(), P(), P(), P(), own),
        out_specs=(P("gx", "gy", None), P(("gx", "gy"), None, None, None)),
        check_vma=False,
    )
```

```python
import functools
import numpy as np
import jax, jax.numpy as jnp
from jax import lax
from jax.experimental import pallas as pl
from jax.experimental.pallas import tpu as pltpu
from jax.sharding import PartitionSpec as P
F32, BF = jnp.float32, jnp.bfloat16
NP, NK, NO, H, A = 90, 24, 16, 256, 256
PR = 96
G = 16
NT = (((1,), (1,)), ((), ()))

def dot(a, b):
    return jnp.dot(a, b, preferred_element_type=F32)
def dot_nt(a, b):
    return lax.dot_general(a, b, NT, preferred_element_type=F32)

def diag(x, y):
    z = jnp.zeros_like(x)
    return jnp.concatenate([jnp.concatenate([x, z], 1), jnp.concatenate([z, y], 1)], 0)

def k1_body(unroll, nbr, ext, sel, corr, w1_hbm, b1, w2, b2, w3, b3, ro, e_ref, s_hbm, o_ref,
            table, tmp, mask, d_ref, w1, wide, rows, w_sem, s_sem):
    step = pl.program_id(0)
    fetch = pltpu.make_async_copy(w1_hbm, w1, w_sem)
    @pl.when(step == 0)
    def _():
        fetch.start()
        tmp[pl.ds(270 * 16, 18 * 16), :] = jnp.zeros((18 * 16, 128), F32)
        lane = lax.broadcasted_iota(jnp.int32, (16, 128), 1) >> 4
        for kk in range(8):
            mask[kk] = jnp.where(lane == kk, 1.0, 0.0).astype(BF)
        @pl.loop(0, 9)
        def _(b):
            own = ext[pl.ds(pl.multiple_of(b * 256, 256), 256), :]
            for o in range(0, 16, 2):
                t = dot(own, sel[:, o * 128:(o + 2) * 128])
                for h in range(2):
                    tmp[pl.ds(o + h, 256, stride=16), :] = t[:, h * 128:(h + 1) * 128]
            table[pl.ds(b * 256, 256)] = tmp[pl.ds(0, 4096), :].reshape(256, 16, 128).astype(BF)
    @pl.loop(0, 10)
    def _(c):
        for r in range(27):
            x = corr[:, pl.ds(pl.multiple_of((c * 27 + r) * 128, 128), 128)].astype(F32)
            tmp[pl.ds(pl.multiple_of((c * 27 + r) * 16, 16), 16), :] = x
    pad = jnp.zeros((128 - PR, 128), BF)
    d2 = d_ref.reshape(PR * A, 128)
    def bdiag(i, h, j):
        base = (step * G + 2 * i + h) * NK + 8 * j
        return jnp.concatenate([table[nbr[base + kk]] * mask[kk] for kk in range(8)], 0)
    def pair(i):
        o = [[tmp[pl.ds(j * 16 + 2 * i + h, PR, stride=48), :].astype(BF) for j in range(3)] for h in range(2)]
        ot = [[jnp.concatenate([o[h][j], pad], 0).T for j in range(3)] for h in range(2)]
        p = []
        for j in range(3):
            both = jnp.concatenate([o[0][j], o[1][j]], 1)
            o_ref[i, :, j * 256:(j + 1) * 256] = both
            p.append(dot(both, diag(bdiag(i, 0, j), bdiag(i, 1, j))).astype(BF))
        d = dot(jnp.concatenate(p, 1), jnp.concatenate([diag(ot[0][j], ot[1][j]) for j in range(3)], 0))
        for h in range(2):
            d2[pl.ds(step * G + 2 * i + h, PR, stride=A), :] = d[:, h * 128:(h + 1) * 128]
    @pl.loop(0, G // 2 // unroll)
    def _(i):
        for u in range(unroll):
            pair(i * unroll + u)
    @pl.when(step == pl.num_programs(0) - 1)
    def _():
        fetch.wait()
        gap = jnp.zeros((128 - PR, H), BF)
        t = jnp.zeros((A, H), F32)
        for c in range(PR // PC):
            n = min(PC * NP, NP * NP - c * PC * NP)
            rows[:n, :] = w1[c * PC * NP:c * PC * NP + n, :].astype(F32)
            rows[n:n + 8, :] = jnp.zeros((8, H), F32)
            for v in range(0, n // NP, 2):
                w = [rows[NP * u:NP * u + PR, :].astype(BF) for u in (v, v + 1)]
                w = jnp.concatenate([w[0], gap, w[1], gap], 0)
                p = c * PC + v
                wide[p // 2] = w
                t = t + dot(jnp.concatenate([d_ref[p], d_ref[p + 1]], 1).astype(BF), w)
        act1 = jnp.tanh(t + b1[...])
        th2 = jnp.tanh(dot(act1.astype(BF), w2[...]) + b2[...])
        act2 = act1 + th2
        th3 = jnp.tanh(dot(act2.astype(BF), w3[...]) + b3[...])
        e_ref[...] = jnp.sum(((act2 + th3) * ro[...]).T, axis=0, keepdims=True)
        g3 = (ro[...] * (1.0 - th3 * th3)).astype(BF)
        back2 = ro[...] + dot_nt(g3, w3[...])
        g2 = (back2 * (1.0 - th2 * th2)).astype(BF)
        back1 = back2 + dot_nt(g2, w2[...])
        g1 = (back1 * (1.0 - act1 * act1)).astype(BF)
        out = []
        for c in range(PR // PC):
            for p in range(c * PC, (c + 1) * PC, 2):
                if p < NP:
                    r = dot_nt(g1, wide[p // 2])
                    d_ref[p] = r[:, :128]
                    d_ref[p + 1] = r[:, 128:]
            here = pl.ds(c * PC, PC)
            out.append(pltpu.make_async_copy(d_ref.at[here], s_hbm.at[here], s_sem.at[c]))
            out[-1].start()
        for copy in out:
            copy.wait()

PC = 16
def k1(nbr, ext, sel, corr, w1, b1, w2, b2, w3, b3, ro, unroll=8):
    row = lambda: pl.BlockSpec((1, H), lambda s, n: (0, 0))
    mat = lambda: pl.BlockSpec((H, H), lambda s, n: (0, 0))
    return pl.pallas_call(
        functools.partial(k1_body, unroll),
        grid_spec=pltpu.PrefetchScalarGridSpec(
            num_scalar_prefetch=1, grid=(A // G,),
            in_specs=[pl.BlockSpec((9 * A, 256), lambda s, n: (0, 0)),
                      pl.BlockSpec((256, 2048), lambda s, n: (0, 0)),
                      pl.BlockSpec((G, 34560), lambda s, n: (s, 0)),
                      pl.BlockSpec(memory_space=pl.ANY),
                      row(), mat(), row(), mat(), row(), row()],
            out_specs=[pl.BlockSpec((1, A), lambda s, n: (0, 0)),
                       pl.BlockSpec(memory_space=pl.ANY),
                       pl.BlockSpec((G // 2, PR, 768), lambda s, n: (s, 0, 0))],
            scratch_shapes=[pltpu.VMEM((9 * A, 16, 128), BF), pltpu.VMEM((288 * 16, 128), F32),
                            pltpu.VMEM((8, 16, 128), BF),
                            pltpu.VMEM((PR, A, 128), F32), pltpu.VMEM((NP * NP, H), BF),
                            pltpu.VMEM((NP // 2, 256, H), BF), pltpu.VMEM((PC * NP + 8, H), F32),
                            pltpu.SemaphoreType.DMA, pltpu.SemaphoreType.DMA((PR // PC,))]),
        out_shape=[jax.ShapeDtypeStruct((1, A), F32), jax.ShapeDtypeStruct((PR, A, 128), F32),
                   jax.ShapeDtypeStruct((A // 2, PR, 768), BF)],
        compiler_params=pltpu.CompilerParams(vmem_limit_bytes=60 << 20, dimension_semantics=("arbitrary",)),
        name="descriptor",
    )(nbr, ext, sel, corr, w1, b1, w2, b2, w3, b3, ro)

def consts():
    i = np.arange(256)[:, None]; c = np.arange(2048)[None]
    sel = (((i >> 4) == (c >> 7)) & ((i & 15) == (c & 15))).astype(BF)
    return jnp.asarray(sel)

def relay(corr):
    return corr.reshape(256, 34560)

def k3_body(unroll, nbr, s_ref, o_ref, fold, out_ref, acc):
    step = pl.program_id(0)
    @pl.when(step == 0)
    def _():
        @pl.loop(0, 144)
        def _(c):
            acc[pl.ds(c * 16, 16)] = jnp.zeros((16, 16, 128), F32)
    s2 = s_ref.reshape(PR * G, 128)
    pad = jnp.zeros((128 - PR, 128), BF)
    lane = lax.broadcasted_iota(jnp.int32, (16, 128), 1) // 16
    def pair(i):
        st = [jnp.concatenate([s2[pl.ds(2 * i + h, PR, stride=G), :].astype(BF), pad], 0).T for h in range(2)]
        o = [[jnp.concatenate([o_ref[i, :, j * 256 + h * 128:j * 256 + h * 128 + 128], pad], 0) for j in range(3)] for h in range(2)]
        ot = jnp.concatenate([jnp.concatenate([o[0][j].T, o[1][j].T], 1) for j in range(3)], 0)
        lt = dot(ot, diag(*st)).astype(BF)
        for j in range(3):
            r = dot(lt[j * 128:(j + 1) * 128], diag(o[0][j], o[1][j]))
            for h in range(2):
                base = (step * G + 2 * i + h) * NK + 8 * j
                ns = [nbr[base + kk] for kk in range(8)]
                new = [acc[ns[kk]] + r[kk * 16:(kk + 1) * 16, h * 128:(h + 1) * 128] for kk in range(8)]
                for kk in range(8):
                    pltpu.store(acc.at[ns[kk]], new[kk], mask=lane == kk)
    @pl.loop(0, G // 2 // unroll)
    def _(i):
        for u in range(unroll):
            pair(i * unroll + u)
    @pl.when(step == pl.num_programs(0) - 1)
    def _():
        acc2 = acc.reshape(9 * A * 16, 128)
        @pl.loop(0, 9)
        def _(b):
            t = dot(jnp.concatenate([acc2[pl.ds(b * 4096 + q, 256, stride=16), :].astype(BF) for q in range(16)], 1), fold[...])
            out_ref[pl.ds(pl.multiple_of(b * 256, 256), 256), :] = t.astype(BF)

def k3(nbr, s, ot, fold, unroll=1):
    return pl.pallas_call(
        functools.partial(k3_body, unroll),
        grid_spec=pltpu.PrefetchScalarGridSpec(
            num_scalar_prefetch=1, grid=(A // G,),
            in_specs=[pl.BlockSpec((PR, G, 128), lambda s, n: (0, s, 0)),
                      pl.BlockSpec((G // 2, PR, 768), lambda s, n: (s, 0, 0)),
                      pl.BlockSpec((2048, 256), lambda s, n: (0, 0))],
            out_specs=pl.BlockSpec((9 * A, 256), lambda s, n: (0, 0)),
            scratch_shapes=[pltpu.VMEM((9 * A, 16, 128), F32)]),
        out_shape=jax.ShapeDtypeStruct((9 * A, 256), BF),
        compiler_params=pltpu.CompilerParams(vmem_limit_bytes=60 << 20),
        name="hamilton",
    )(nbr, s, ot, fold)

def fold_of():
    i = np.arange(2048)[:, None]; c = np.arange(256)[None]
    return jnp.asarray((((i >> 7) == (c & 15)) & ((i & 15) == (c >> 4))).astype(BF))


MESH = pl.DeviceIdType.MESH


def greet(peers):
    barrier = pltpu.get_barrier_semaphore()
    for peer in peers:
        pl.semaphore_signal(barrier, inc=1, device_id=peer, device_id_type=MESH)
    pl.semaphore_wait(barrier, len(peers))


def push(src, dst, send, recv, peer):
    copy = pltpu.make_async_remote_copy(src_ref=src, dst_ref=dst, send_sem=send, recv_sem=recv,
                                        device_id=peer, device_id_type=MESH)
    copy.start()
    return copy


def halo_body(nx, ny, own, out, sy, ry, sx, rx):
    x, y = lax.axis_index("gx"), lax.axis_index("gy")
    onx = lambda k: {"gx": lax.rem(x + k + nx, nx)}
    ony = lambda k: {"gy": lax.rem(y + k + ny, ny)}
    greet([onx(1), onx(-1), ony(1), ony(-1)])
    out[1, 1] = own[...]
    first = [push(own, out.at[1, 1 - k], sy.at[(k + 1) // 2], ry.at[(k + 1) // 2], ony(k)) for k in (1, -1)]
    second = []
    def spread(j):
        for k in (1, -1):
            second.append(push(own if j == 1 else out.at[1, j], out.at[1 - k, j],
                               sx.at[(k + 1) // 2, j], rx.at[(k + 1) // 2, j], onx(k)))
    spread(1)
    for k, copy in zip((1, -1), first):
        copy.wait_recv()
        spread(1 - k)
    for copy in second:
        copy.wait_recv()
    for copy in first + second:
        copy.wait_send()


def halo(own, nx, ny):
    dma = pltpu.SemaphoreType.DMA
    return pl.pallas_call(
        functools.partial(halo_body, nx, ny),
        out_shape=jax.ShapeDtypeStruct((3, 3, A, 256), BF),
        in_specs=[pl.BlockSpec(memory_space=pltpu.VMEM)],
        out_specs=pl.BlockSpec(memory_space=pltpu.VMEM),
        scratch_shapes=[dma((2,)), dma((2,)), dma((2, 3)), dma((2, 3))],
        compiler_params=pltpu.CompilerParams(collective_id=0, has_side_effects=True),
        name="halo",
    )(own)


def exchange_body(nx, ny, part, pos, out, mine, near, edge, far, chosen, sent, mid, sm, s1, r1, s2, r2, s3, r3, s4, r4):
    x, y = lax.axis_index("gx"), lax.axis_index("gy")
    onx = lambda k: {"gx": lax.rem(x + k + nx, nx)}
    ony = lambda k: {"gy": lax.rem(y + k + ny, ny)}
    take = pltpu.make_async_copy(part.at[1], mine, sm)
    take.start()
    greet([onx(k) for k in range(1, nx)] + [ony(k) for k in range(1, ny)])
    first = {}
    for j in (0, 2, 1):
        for d, k in enumerate((1, -1)):
            first[d, j] = push(part.at[1 + k, j], near.at[d, j], s1.at[d, j], r1.at[d, j], onx(k))
    rows = nx * ny * 8
    r = lax.broadcasted_iota(jnp.int32, (rows, A), 0)
    hit = ((r >> 3) * 4 + (r & 3)) == pos[...]
    half = (r >> 2) & 1
    for h in range(2):
        chosen[:, h * A:(h + 1) * A] = jnp.where(hit & (half == h), 1.0, 0.0).astype(BF)

    take.wait()

    def fold(j):
        first[0, j].wait_recv()
        first[1, j].wait_recv()
        return mine[j].astype(F32) + near[0, j].astype(F32) + near[1, j].astype(F32)
    second = []
    for d, (j, k) in enumerate(((2, 1), (0, -1))):
        edge[d] = fold(j).astype(BF)
        second.append(push(edge.at[d], far.at[d], s2.at[d], r2.at[d], ony(k)))
    total = fold(1)
    for d in range(2):
        second[d].wait_recv()
        total = total + far[d].astype(F32)
    both = jnp.concatenate([total[:, :128], total[:, 128:]], 0).astype(BF)
    sent[...] = dot(chosen[...], both).reshape(nx, ny, 8, 128).astype(BF)
    third = [push(sent.at[lax.rem(x + k, nx)], mid.at[x], s3.at[k], r3.at[k], onx(k)) for k in range(1, nx)]
    mid[x] = sent[x]
    for copy in third:
        copy.wait_recv()
    fourth = [push(mid.at[:, lax.rem(y + k, ny)], out.at[:, y], s4.at[k], r4.at[k], ony(k)) for k in range(1, ny)]
    out[:, y] = mid[:, y]
    for copy in fourth:
        copy.wait_recv()
    for copy in list(first.values()) + second + third + fourth:
        copy.wait_send()


def exchange(part, position, nx, ny):
    dma = pltpu.SemaphoreType.DMA
    vmem = pl.BlockSpec(memory_space=pltpu.VMEM)
    return pl.pallas_call(
        functools.partial(exchange_body, nx, ny),
        out_shape=jax.ShapeDtypeStruct((nx, ny, 8, 128), BF),
        in_specs=[pl.BlockSpec(memory_space=pl.ANY), vmem], out_specs=vmem,
        scratch_shapes=[pltpu.VMEM((3, A, 256), BF), pltpu.VMEM((2, 3, A, 256), BF), pltpu.VMEM((2, A, 256), BF), pltpu.VMEM((2, A, 256), BF),
                        pltpu.VMEM((nx * ny * 8, 2 * A), BF), pltpu.VMEM((nx, ny, 8, 128), BF),
                        pltpu.VMEM((nx, ny, 8, 128), BF),
                        dma, dma((2, 3)), dma((2, 3)), dma((2,)), dma((2,)), dma((nx,)), dma((nx,)), dma((ny,)), dma((ny,))],
        compiler_params=pltpu.CompilerParams(collective_id=1, has_side_effects=True, vmem_limit_bytes=63 << 20),
        name="exchange",
    )(part, position)


def on_device(density, neighbours, correlations, weight_first, bias_first, weight_second, bias_second,
              weight_third, bias_third, readout, destination):
    nx, ny = lax.axis_size("gx"), lax.axis_size("gy")
    sel = consts()
    nbr = neighbours.reshape(A * NK)
    ext = halo(density.reshape(A, 256), nx, ny).reshape(9 * A, 256)
    row = lambda v: v.reshape(1, H)
    energy, slope, o = k1(nbr, ext, sel, relay(correlations), weight_first, row(bias_first), weight_second,
                          row(bias_second), weight_third, row(bias_third), row(readout))
    part = k3(nbr, slope, o, fold_of(), 8).reshape(3, 3, A, 256)
    target = destination.reshape(A)
    order = jnp.arange(A, dtype=jnp.int32)
    earlier = (target[:, None] == target[None, :]) & (order[:, None] < order[None, :])
    position = target * 4 + jnp.sum(earlier.astype(jnp.int32), axis=0)
    received = exchange(part, position.reshape(1, A), nx, ny)
    blocks = received.reshape(nx * ny, 2, 4, 128).transpose(0, 2, 1, 3).reshape(1, nx * ny, 4, 256).astype(F32)
    return energy.reshape(1, 1, A), blocks


def solution(mesh):
    own = P("gx", "gy", None, None)
    return jax.shard_map(
        on_device,
        mesh=mesh,
        in_specs=(own, own, own, P(), P(), P(), P(), P(), P(), P(), own),
        out_specs=(P("gx", "gy", None), P(("gx", "gy"), None, None, None)),
        check_vma=False,
    )
```
